128 devices in a mesh: gx: 32 (over y, z, core), gy: 4 (over x).
Axes of the slice: x: 4, y: 4, z: 4, core: 2. Of those that a mesh axis runs over, the one named last changes fastest.
Arguments:
- cotangent: float32 [9, 256, 256, 256], P(None, 'gx', 'gy'), may hold values from -6 to 6
- fields_one: float32 [9, 256, 256, 256], P(None, 'gx', 'gy'), may hold values from 0 to 1
- fields_zero: float32 [9, 256, 256, 256], P(None, 'gx', 'gy'), may hold values from 0 to 1
- slot_grain: int32 [32, 32, 8], P('gx', 'gy'), may hold values from 0 to 1023, as said below
Outputs:
- adjoint_fields: float32 [9, 256, 256, 256], P(None, 'gx', 'gy')
- grain_grad: float32 [1024, 256], P(('gx', 'gy'))
The draws below stay inside these ranges and needn't reach their ends.
Inputs may be any that keep to these rules, and one draw needn't show every extreme that they name: `slot_grain`: grain g is owned by device g // 8, devices counted with gx slowest. Every slot of a tile names a grain whose owner has the tile's index along gy. At most 4 of the slots of one device name grains of one owner, and in every draw some owner receives exactly 4 from every device of its gy group.
All inputs are finite; a program needn't handle non-finite values.
Results may differ from the reference program's by a relative error of at most 0.000096.
Values sent between devices are 32-bit elements; how exact they have to be, the bound alone decides.
No kernel may reach another device: no remote copies, remote signals or barrier semaphores. Data moves between devices by JAX's collectives and lax.ppermute only.
A program may use at most 128 MiB of HBM per device.

```python
import jax
import jax.numpy as jnp
from jax import lax

SLOTS = 8
TILE = 8
CX = 8
CY = 64
NZ = 256
GRAIN_DEV = 8
NX = 256
NY = 256
GRAINS = 1024
ROWS_DEV = 64
CAP = 4
N_GX = 32
N_GY = 4


def draw_slot_grain(key, part):
    peer_count = N_GX
    groups = N_GY
    key_full, key_rows, key_local = jax.random.split(key, 3)
    full_peer = jax.random.randint(key_full, (groups,), 0, peer_count)
    full_each = jnp.tile(full_peer, peer_count)

    def one_device(device_key, chosen_peer):
        key_rank, key_shuffle = jax.random.split(device_key)
        ranks = jax.random.permutation(key_rank, peer_count * CAP)
        candidate = jnp.arange(peer_count * CAP)
        scores = ranks + jnp.where(candidate // CAP == chosen_peer, peer_count * CAP, 0)
        scores_top, picked = lax.top_k(scores, ROWS_DEV)
        picked = jax.random.permutation(key_shuffle, picked)
        return picked // CAP
    device_keys = jax.random.split(key_rows, peer_count * groups)
    peers = jax.vmap(one_device)(device_keys, full_each)
    local_id = jax.random.randint(key_local, (peer_count * groups, ROWS_DEV), 0, GRAIN_DEV)
    group_index = jnp.arange(peer_count * groups) % groups
    grains = (peers * groups + group_index[:, None]) * GRAIN_DEV + local_id
    grains = grains.reshape(peer_count, groups, CX // TILE, CY // TILE, SLOTS)
    grains = jnp.transpose(grains, (0, 2, 1, 3, 4))
    return grains.reshape(NX // TILE, NY // TILE, SLOTS).astype(jnp.int32)


def levels(own_key, dims, shards, low, largest):
    factor_of, own = 1.0, jax.random.fold_in(own_key, 6)
    for position, parts in shards:
        draws = jnp.exp(jax.random.uniform(jax.random.fold_in(own, position), (parts,), jnp.float32, low / len(shards), largest / len(shards)))
        factor_of = factor_of * jnp.repeat(draws, dims[position] // parts).reshape([-1 if axis == position else 1 for axis in range(len(dims))])
    return factor_of


def gaussian(stream_key, extent, spread, limit, shards=(), kind=jnp.bfloat16):
    drawn = spread * jax.random.normal(stream_key, extent, jnp.float32)
    if shards:
        drawn = drawn * levels(stream_key, extent, shards, -0.22, 0.18)
    return jnp.clip(drawn, -limit, limit).astype(kind)


def setup_inputs(seed: int = 0) -> dict:
    splits = jax.random.split(jax.random.key(seed), 5)
    cotangent = gaussian(splits[0], (SLOTS + 1, NX, NY, NZ), 1.0, 6.0, ((1, 32), (2, 4)), jnp.float32)
    fields_one = jnp.clip(1.0 * jax.random.uniform(splits[1], (SLOTS + 1, NX, NY, NZ), jnp.float32) ** levels(splits[1], (SLOTS + 1, NX, NY, NZ), ((1, 32), (2, 4)), -0.2, 0.2), 0.0, 1.0)
    fields_zero = jnp.clip(1.0 * jax.random.uniform(splits[2], (SLOTS + 1, NX, NY, NZ), jnp.float32) ** levels(splits[2], (SLOTS + 1, NX, NY, NZ), ((1, 32), (2, 4)), -0.2, 0.2), 0.0, 1.0)
    slot_grain = draw_slot_grain(jax.random.fold_in(splits[4], 71), 0)
    return {"cotangent": cotangent, "fields_one": fields_one, "fields_zero": fields_zero, "slot_grain": slot_grain}


time_step = 0.05
well_height = 16.0
barrier = 1.0


def laplace(value):
    extended = jnp.pad(value, [(0, 0)] * (value.ndim - 3) + [(1, 1)] * 3)
    total = extended[..., 2:, 1:-1, 1:-1] + extended[..., :-2, 1:-1, 1:-1]
    total = total + extended[..., 1:-1, 2:, 1:-1] + extended[..., 1:-1, :-2, 1:-1]
    total = total + extended[..., 1:-1, 1:-1, 2:] + extended[..., 1:-1, 1:-1, :-2]
    return total - 6.0 * value


def pointwise(costate, fields, lap_costate, lam_mu, lap_mu):
    density = fields[0]
    phases = fields[1:]
    lam_c = costate[0]
    lam_e = costate[1:]
    square_sum = jnp.sum(phases * phases, axis=0)
    weighted = jnp.sum(lam_e * phases, axis=0)
    coupled = jnp.sum(lam_e * (phases * phases - phases), axis=0)
    curvature = well_height * (2.0 - 12.0 * density + 12.0 * density * density) + 2.0 * barrier
    new_density = lam_c + lam_mu * curvature - lap_mu - 12.0 * barrier * time_step * coupled
    inner = lam_e * ((1.0 - density) - 2.0 * (2.0 - density) * phases + square_sum) + 2.0 * phases * weighted
    new_phases = lam_e - 12.0 * barrier * time_step * inner + time_step * lap_costate[1:]
    new_phases = new_phases + 12.0 * barrier * lam_mu * (phases * phases - phases)
    return jnp.concatenate([new_density[None], new_phases], axis=0)


def adjoint_step(costate, fields):
    lap_costate = laplace(costate)
    lam_mu = time_step * lap_costate[0]
    lap_mu = laplace(lam_mu)
    return pointwise(costate, fields, lap_costate, lam_mu, lap_mu)


def tile_rows(phase_costate):
    slots, size_x, size_y, depth = phase_costate.shape
    blocks = phase_costate.reshape(slots, size_x // TILE, TILE, size_y // TILE, TILE, depth)
    summed = jnp.sum(blocks, axis=(2, 4))
    return jnp.transpose(summed, (1, 2, 0, 3)).reshape(-1, depth)


def reference(cotangent, fields_one, fields_zero, slot_grain):
    costate_one = adjoint_step(cotangent, fields_one)
    adjoint_fields = adjoint_step(costate_one, fields_zero)
    partial_value = time_step * tile_rows(cotangent[1:]) + time_step * tile_rows(costate_one[1:])
    grain_grad = jax.ops.segment_sum(partial_value, slot_grain.reshape(-1).astype(jnp.int32), num_segments=GRAINS)
    return adjoint_fields, grain_grad
```

```python
import functools

import jax
import jax.numpy as jnp
from jax import lax
from jax.experimental import pallas as pl
from jax.experimental.pallas import tpu as pltpu
from jax.sharding import PartitionSpec as P

DT = 0.05
SLOTS = 8
NF = SLOTS + 1
CX, CY, NZ = 8, 64, 256
LN = 128
HALF = NZ // LN
GRAIN_DEV = 8
PAD = 8
ROWS = CY + 2 * PAD
FACE = (SLOTS + 2) * CY
FACE_ROWS = FACE + 8
SIDE_ROWS = (SLOTS + 2) * CX
F32 = jnp.float32
ANY = pl.BlockSpec(memory_space=pl.ANY)
VM = pl.BlockSpec(memory_space=pltpu.VMEM)
SM = pl.BlockSpec(memory_space=pltpu.SMEM)


def lanes(half):
    return slice(half * LN, (half + 1) * LN)


def z_sum(first, second):
    lane = lax.broadcasted_iota(jnp.int32, first.shape, first.ndim - 1)
    axis = first.ndim - 1
    low, high = lane == 0, lane == LN - 1
    from_low = pltpu.roll(first, 1, axis)
    from_high = pltpu.roll(second, LN - 1, axis)
    left = jnp.where(low, 0.0, from_low), jnp.where(low, from_low, pltpu.roll(second, 1, axis))
    right = jnp.where(high, from_high, pltpu.roll(first, LN - 1, axis)), jnp.where(high, 0.0, from_high)
    return left[0] + right[0], left[1] + right[1]


def start_all(copies):
    for copy in copies:
        copy.start()
    return copies


def wait_all(copies):
    for copy in copies:
        copy.wait()


def local_kernel(with_sums, cos, fld, out, *rest):
    if with_sums:
        sums, value, field, result, potential, sem_c, sem_e, sem_f, sem_o = rest
    else:
        value, field, result, potential, sem_c, sem_e, sem_f, sem_o = rest
        sums = None

    def copy_c(h):
        return pltpu.make_async_copy(
            cos.at[0, :, :, lanes(h)], value.at[0, h, 1 : CX + 1, PAD : PAD + CY, :], sem_c.at[h]
        )

    def copy_e(x, h):
        return pltpu.make_async_copy(
            cos.at[1:NF, x, :, lanes(h)],
            value.at[1:NF, h, x + 1, PAD : PAD + CY, :],
            sem_e.at[x, h],
        )

    def copy_f(x, h):
        return pltpu.make_async_copy(fld.at[:, x, :, lanes(h)], field.at[:, h, x], sem_f.at[x, h])

    def copy_o(x, h):
        return pltpu.make_async_copy(result.at[:, h, x], out.at[:, x, :, lanes(h)], sem_o.at[x, h])

    for h in range(HALF):
        copy_c(h).start()
    for x in range(CX):
        for h in range(HALF):
            copy_e(x, h).start()
            copy_f(x, h).start()

    tile = jnp.zeros((8, LN), F32)
    plane = jnp.zeros((CY, LN), F32)
    for h in range(HALF):
        for ref in [value.at[s] for s in range(NF)] + [potential]:
            ref[h, 0, PAD : PAD + CY, :] = plane
            ref[h, CX + 1, PAD : PAD + CY, :] = plane
            for x in range(1, CX + 1):
                ref[h, x, 0:PAD, :] = tile
                ref[h, x, PAD + CY : ROWS, :] = tile
    if sums is not None:
        sums[...] = jnp.zeros(sums.shape, F32)

    def around(ref, x, row):
        own = [ref[h, x + 1, row : row + 8, :] for h in range(HALF)]
        along_z = z_sum(*own)
        total = [
            (ref[h, x, row : row + 8, :] + ref[h, x + 2, row : row + 8, :])
            + (ref[h, x + 1, row - 1 : row + 7, :] + ref[h, x + 1, row + 1 : row + 9, :])
            + along_z[h]
            for h in range(HALF)
        ]
        return own, total

    for h in range(HALF):
        copy_c(h).wait()

    def potential_plane(x, carry):
        for part in range(CY // 8):
            row = PAD + part * 8
            own, total = around(value.at[0], x, row)
            for h in range(HALF):
                potential[h, x + 1, row : row + 8, :] = DT * total[h] - (6.0 * DT) * own[h]
        return carry

    lax.fori_loop(0, CX, potential_plane, 0)

    for h in range(HALF):
        copy_e(0, h).wait()

    def step_plane(x, carry):
        @pl.when(x < CX - 1)
        def _():
            for h in range(HALF):
                copy_e(x + 1, h).wait()

        for h in range(HALF):
            copy_f(x, h).wait()
        for part in range(CY // 8):
            row = PAD + part * 8
            here = slice(part * 8, part * 8 + 8)
            both = range(HALF)
            square = [None] * HALF
            weighted = [None] * HALF
            curved = [None] * HALF
            for s in range(1, NF):
                for h in both:
                    eta = field[s, h, x, here, :]
                    lam = value[s, h, x + 1, row : row + 8, :]
                    eta_eta = eta * eta
                    lam_eta = lam * eta
                    cubic = lam_eta * eta
                    square[h] = eta_eta if square[h] is None else square[h] + eta_eta
                    weighted[h] = lam_eta if weighted[h] is None else weighted[h] + lam_eta
                    curved[h] = cubic if curved[h] is None else curved[h] + cubic
            mu, mu_total = around(potential, x, row)
            scale, slope, mu_twelve, linear = [], [], [], []
            for h in both:
                density = field[0, h, x, here, :]
                lam_c = value[0, h, x + 1, row : row + 8, :]
                curvature = 34.0 + density * (192.0 * density - 192.0)
                result[0, h, x, here, :] = (
                    lam_c
                    + mu[h] * (curvature + 6.0)
                    - mu_total[h]
                    - (12.0 * DT) * (curved[h] - weighted[h])
                )
                scale.append((1.0 - 18.0 * DT) + (12.0 * DT) * (density - square[h]))
                slope.append((48.0 * DT) - (24.0 * DT) * density)
                mu_twelve.append(12.0 * mu[h])
                linear.append((24.0 * DT) * weighted[h] + mu_twelve[h])
            for s in range(1, NF):
                lam, total = around(value.at[s], x, row)
                for h in both:
                    eta = field[s, h, x, here, :]
                    new = (
                        lam[h] * (scale[h] + slope[h] * eta)
                        + eta * (mu_twelve[h] * eta - linear[h])
                        + DT * total[h]
                    )
                    result[s, h, x, here, :] = new
                    if sums is not None:
                        sums[s - 1, h, here, :] += lam[h] + new
        for h in range(HALF):
            copy_o(x, h).start()
        return carry

    lax.fori_loop(0, CX, step_plane, 0)
    for x in range(CX):
        for h in range(HALF):
            copy_o(x, h).wait()


def local_step(cos, fld, with_sums):
    out_shape = [jax.ShapeDtypeStruct((NF, CX, CY, NZ), F32)]
    out_specs = [ANY]
    if with_sums:
        out_shape.append(jax.ShapeDtypeStruct((SLOTS, HALF, CY, LN), F32))
        out_specs.append(VM)
    return pl.pallas_call(
        functools.partial(local_kernel, with_sums),
        out_shape=out_shape,
        in_specs=[ANY, ANY],
        out_specs=out_specs,
        scratch_shapes=[
            pltpu.VMEM((NF, HALF, CX + 2, ROWS, LN), F32),
            pltpu.VMEM((NF, HALF, CX, CY, LN), F32),
            pltpu.VMEM((NF, HALF, CX, CY, LN), F32),
            pltpu.VMEM((HALF, CX + 2, ROWS, LN), F32),
            pltpu.SemaphoreType.DMA((HALF,)),
            pltpu.SemaphoreType.DMA((CX, HALF)),
            pltpu.SemaphoreType.DMA((CX, HALF)),
            pltpu.SemaphoreType.DMA((CX, HALF)),
        ],
        compiler_params=pltpu.CompilerParams(vmem_limit_bytes=28 << 20),
        cost_estimate=pl.CostEstimate(flops=250 * CX * CY * NZ, bytes_accessed=3 * 4 * NF * CX * CY * NZ, transcendentals=0),
        name="local_step",
    )(cos, fld)


def pack_kernel(place, cos, face_a, face_b, side_a, side_b, tiles, sem_p, sem_t):
    even_x = place[0] == 0
    even_y = place[1] == 0
    out_a = jnp.where(even_x, CX - 1, 0)
    in_a = jnp.where(even_x, CX - 2, 1)
    loads = start_all(
        [
            pltpu.make_async_copy(
                cos.at[:, :, edge * (CY - 8) : edge * (CY - 8) + 8, :], tiles.at[edge], sem_t.at[edge]
            )
            for edge in range(2)
        ]
    )
    copies = []
    for which, face, outer, inner in ((0, face_a, out_a, in_a), (1, face_b, CX - 1 - out_a, CX - 1 - in_a)):
        for h in range(HALF):
            for k in range(SLOTS + 2):
                s = k + 1 if k < SLOTS else 0
                x = inner if k == SLOTS + 1 else outer
                copies.append(
                    pltpu.make_async_copy(
                        cos.at[s, x, :, lanes(h)],
                        face.at[h, k * CY : (k + 1) * CY, :],
                        sem_p.at[which, h, k],
                    )
                )
    start_all(copies)
    wait_all(loads)
    for h in range(HALF):
        for k in range(SLOTS + 2):
            s = k + 1 if k < SLOTS else 0
            depth = 1 if k == SLOTS + 1 else 0
            low = tiles[0, s, :, depth, lanes(h)]
            high = tiles[1, s, :, 7 - depth, lanes(h)]
            side_a[h, k * CX : (k + 1) * CX, :] = jnp.where(even_y, high, low)
            side_b[h, k * CX : (k + 1) * CX, :] = jnp.where(even_y, low, high)
    wait_all(copies)


def pack(place, cos):
    face = jax.ShapeDtypeStruct((HALF, FACE_ROWS, LN), F32)
    side = jax.ShapeDtypeStruct((HALF, SIDE_ROWS, LN), F32)
    return pl.pallas_call(
        pack_kernel,
        out_shape=[face, face, side, side],
        in_specs=[SM, ANY],
        out_specs=[ANY, ANY, VM, VM],
        scratch_shapes=[
            pltpu.VMEM((2, NF, CX, 8, NZ), F32),
            pltpu.SemaphoreType.DMA((2, HALF, SLOTS + 2)),
            pltpu.SemaphoreType.DMA((2,)),
        ],
        compiler_params=pltpu.CompilerParams(vmem_limit_bytes=8 << 20),
        name="pack",
    )(place, cos)


def corner_kernel(place, got_a, got_b, face_a, face_b, out_a, out_b, tiles, sem):
    del face_a, face_b
    even_x = place[0] == 0
    even_y = place[1] == 0
    row = lax.broadcasted_iota(jnp.int32, (8, LN), 0)
    copies = []
    for h in range(HALF):
        here = slice(SLOTS * CX, SLOTS * CX + CX)
        first, second = got_a[h, here, :], got_b[h, here, :]
        low = jnp.where(even_y, second, first)
        high = jnp.where(even_y, first, second)

        def ends(x):
            return jnp.where(row == 0, low[x : x + 1, :], high[x : x + 1, :])

        at_low, at_high = ends(0), ends(CX - 1)
        tiles[0, h] = jnp.where(even_x, at_high, at_low)
        tiles[1, h] = jnp.where(even_x, at_low, at_high)
        for which, out in ((0, out_a), (1, out_b)):
            copies.append(
                pltpu.make_async_copy(tiles.at[which, h], out.at[h, FACE:FACE_ROWS, :], sem.at[which, h])
            )
    start_all(copies)
    wait_all(copies)


def corner(place, got, faces):
    face = jax.ShapeDtypeStruct((HALF, FACE_ROWS, LN), F32)
    return pl.pallas_call(
        corner_kernel,
        out_shape=[face, face],
        in_specs=[SM, VM, VM, ANY, ANY],
        out_specs=[ANY, ANY],
        scratch_shapes=[pltpu.VMEM((2, HALF, 8, LN), F32), pltpu.SemaphoreType.DMA((2, HALF))],
        input_output_aliases={3: 0, 4: 1},
        name="corner",
    )(place, *got, *faces)


def fix_kernel(first_step, place, cos, fld, got_fa, got_fb, got_sa, got_sb, base, *rest):
    if first_step:
        sums_in, out, face_a, face_b, side_a, side_b, sums, work, field, own_c, edge, sem_w, sem_f, sem_c, sem_o = rest
    else:
        out, work, field, own_c, edge, sem_w, sem_f, sem_c, sem_o = rest
        sums = None
    even_x = place[0] == 0
    even_y = place[1] == 0
    del base

    def ring(hbm, vmem, sem, whole):
        parts = []
        count = 0
        for h in range(HALF):
            for x in (0, CX - 1):
                parts.append((hbm.at[:, x, :, lanes(h)], vmem.at[:, h, x], sem.at[count]))
                count += 1
            for y in (0, CY - 8):
                rows = slice(y, y + 8)
                first = 0 if whole else 1
                parts.append(
                    (
                        hbm.at[first:NF, 1 : CX - 1, rows, lanes(h)],
                        vmem.at[first:NF, h, 1 : CX - 1, rows, :],
                        sem.at[count],
                    )
                )
                count += 1
                if not whole:
                    parts.append(
                        (
                            hbm.at[0, 2 : CX - 2, rows, lanes(h)],
                            vmem.at[0, h, 2 : CX - 2, rows, :],
                            sem.at[count],
                        )
                    )
                    count += 1
            if not whole:
                for x in (1, CX - 2):
                    parts.append((hbm.at[0, x, :, lanes(h)], vmem.at[0, h, x], sem.at[count]))
                    count += 1
        return parts

    loads = [pltpu.make_async_copy(a, b, c) for a, b, c in ring(out, work, sem_w, False)]
    loads += [pltpu.make_async_copy(a, b, c) for a, b, c in ring(fld, field, sem_f, True)]
    loads += [
        pltpu.make_async_copy(cos.at[0, :, :, lanes(h)], own_c.at[h], sem_c.at[h]) for h in range(HALF)
    ]
    start_all(loads)
    if first_step:
        sums[...] = sums_in[...]
    wait_all(loads)
    both = range(HALF)

    for x, inner, present in ((0, 1, place[2]), (CX - 1, CX - 2, place[3])):

        def got(h, start, size):
            a = got_fa[h, start : start + size, :]
            b = got_fb[h, start : start + size, :]
            return jnp.where(even_x, b, a) if x == 0 else jnp.where(even_x, a, b)

        exists = present.astype(F32) * DT
        delta = []
        for h in both:
            d = DT * got(h, SLOTS * CY, CY)
            ends = DT * got(h, FACE, 8)
            delta.append(d)
            edge[h, 8 : 8 + CY, :] = d
            edge[h, 7:8, :] = ends[0:1, :]
            edge[h, 8 + CY : 9 + CY, :] = ends[1:2, :]
        along_z = z_sum(*delta)
        twelve = []
        for h in both:
            total = along_z[h] + edge[h, 9 : 9 + CY, :] + edge[h, 7 : 7 + CY, :] - 6.0 * delta[h]
            density = field[0, h, x]
            curvature = 34.0 + density * (192.0 * density - 192.0)
            work[0, h, x] += (
                delta[h] * curvature
                - 2.0 * total
                - DT * got(h, (SLOTS + 1) * CY, CY)
                - exists * own_c[h, x]
            )
            work[0, h, inner] -= delta[h]
            twelve.append(12.0 * delta[h])
        for s in range(1, NF):
            for h in both:
                eta = field[s, h, x]
                change = DT * got(h, (s - 1) * CY, CY) + twelve[h] * (eta * eta - eta)
                work[s, h, x] += change
                if sums is not None:
                    sums[s - 1, h] += change

    row = lax.broadcasted_iota(jnp.int32, (CX, LN), 0)
    for y, inner, present in ((0, 1, place[4]), (CY - 1, CY - 2, place[5])):

        def got(h, start):
            a = got_sa[h, start : start + CX, :]
            b = got_sb[h, start : start + CX, :]
            return jnp.where(even_y, b, a) if y == 0 else jnp.where(even_y, a, b)

        exists = present.astype(F32) * DT
        delta = [DT * got(h, SLOTS * CX) for h in both]
        along_z = z_sum(*delta)
        twelve = []
        for h in both:
            d = delta[h]
            along_x = jnp.where(row == 0, 0.0, pltpu.roll(d, 1, 0)) + jnp.where(
                row == CX - 1, 0.0, pltpu.roll(d, CX - 1, 0)
            )
            total = along_z[h] + along_x - 6.0 * d
            density = field[0, h, :, y, :]
            curvature = 34.0 + density * (192.0 * density - 192.0)
            work[0, h, :, y, :] = work[0, h, :, y, :] + (
                d * curvature
                - 2.0 * total
                - DT * got(h, (SLOTS + 1) * CX)
                - exists * own_c[h, :, y, :]
            )
            work[0, h, :, inner, :] = work[0, h, :, inner, :] - d
            twelve.append(12.0 * d)
        for s in range(1, NF):
            for h in both:
                eta = field[s, h, :, y, :]
                change = DT * got(h, (s - 1) * CX) + twelve[h] * (eta * eta - eta)
                work[s, h, :, y, :] = work[s, h, :, y, :] + change
                if sums is not None:
                    sums[s - 1, h, y : y + 1, :] += jnp.sum(change, axis=0, keepdims=True)

    stores = start_all(
        [pltpu.make_async_copy(b, a, c) for a, b, c in ring(out, work, sem_o, False)]
    )
    if first_step:
        for h in both:
            for k in range(SLOTS + 2):
                s = k + 1 if k < SLOTS else 0
                depth = 1 if k == SLOTS + 1 else 0
                low, high = work[s, h, depth], work[s, h, CX - 1 - depth]
                face_a[h, k * CY : (k + 1) * CY, :] = jnp.where(even_x, high, low)
                face_b[h, k * CY : (k + 1) * CY, :] = jnp.where(even_x, low, high)
                low, high = work[s, h, :, depth, :], work[s, h, :, CY - 1 - depth, :]
                side_a[h, k * CX : (k + 1) * CX, :] = jnp.where(even_y, high, low)
                side_b[h, k * CX : (k + 1) * CX, :] = jnp.where(even_y, low, high)
    wait_all(stores)


def fix(place, cos, fld, got_faces, got_sides, base, sums=None):
    first_step = sums is not None
    face = jax.ShapeDtypeStruct((HALF, FACE_ROWS, LN), F32)
    side = jax.ShapeDtypeStruct((HALF, SIDE_ROWS, LN), F32)
    args = [place, cos, fld, *got_faces, *got_sides, base]
    in_specs = [SM, ANY, ANY, VM, VM, VM, VM, ANY]
    out_shape = [jax.ShapeDtypeStruct(base.shape, F32)]
    out_specs = [ANY]
    if first_step:
        args.append(sums)
        in_specs.append(VM)
        out_shape += [face, face, side, side, jax.ShapeDtypeStruct(sums.shape, F32)]
        out_specs += [VM] * 5
    return pl.pallas_call(
        functools.partial(fix_kernel, first_step),
        out_shape=out_shape,
        in_specs=in_specs,
        out_specs=out_specs,
        scratch_shapes=[
            pltpu.VMEM((NF, HALF, CX, CY, LN), F32),
            pltpu.VMEM((NF, HALF, CX, CY, LN), F32),
            pltpu.VMEM((HALF, CX, CY, LN), F32),
            pltpu.VMEM((HALF, ROWS, LN), F32),
            pltpu.SemaphoreType.DMA((16,)),
            pltpu.SemaphoreType.DMA((8,)),
            pltpu.SemaphoreType.DMA((HALF,)),
            pltpu.SemaphoreType.DMA((16,)),
        ],
        input_output_aliases={7: 0},
        compiler_params=pltpu.CompilerParams(vmem_limit_bytes=20 << 20),
        name="halo_fix",
    )(*args)


def grain_kernel(groups, grains, sums, rows):
    rows[...] = jnp.zeros(rows.shape, F32)
    row = lax.broadcasted_iota(jnp.int32, (GRAIN_DEV, LN), 0)
    for t in range(CY // 8):
        for s in range(SLOTS):
            grain = grains[0, t, s]
            start = pl.multiple_of(grain // (GRAIN_DEV * groups) * GRAIN_DEV, GRAIN_DEV)
            chosen = row == grain % GRAIN_DEV
            for h in range(HALF):
                total = DT * jnp.sum(sums[s, h, t * 8 : t * 8 + 8, :], axis=0, keepdims=True)
                rows[pl.ds(start, GRAIN_DEV), lanes(h)] += jnp.where(chosen, total, 0.0)


def grain_rows(slot_grain, sums, peers, groups):
    return pl.pallas_call(
        functools.partial(grain_kernel, groups),
        out_shape=jax.ShapeDtypeStruct((peers * GRAIN_DEV, NZ), F32),
        in_specs=[SM, VM],
        out_specs=VM,
        name="grain_rows",
    )(slot_grain, sums)


def swaps(axis, count, first, second):
    near = [(i, i ^ 1) for i in range(count)]
    far = [(i, ((i + 1) ^ 1) - 1) for i in range(1, count - 1)]
    return lax.ppermute(first, axis, near), lax.ppermute(second, axis, far)


def shards(n_gx, n_gy, cotangent, fields_one, fields_zero, slot_grain):
    gx, gy = lax.axis_index("gx"), lax.axis_index("gy")
    place = jnp.stack(
        [gx % 2, gy % 2, gx > 0, gx < n_gx - 1, gy > 0, gy < n_gy - 1]
    ).astype(jnp.int32)

    def exchange(faces, sides):
        got_sides = swaps("gy", n_gy, *sides)
        faces = corner(place, got_sides, faces)
        return swaps("gx", n_gx, *faces), got_sides

    face_a, face_b, side_a, side_b = pack(place, cotangent)
    got_faces, got_sides = exchange((face_a, face_b), (side_a, side_b))
    base, sums = local_step(cotangent, fields_one, True)
    costate, face_a, face_b, side_a, side_b, sums = fix(
        place, cotangent, fields_one, got_faces, got_sides, base, sums
    )

    got_faces, got_sides = exchange((face_a, face_b), (side_a, side_b))
    rows = grain_rows(slot_grain, sums, n_gx, n_gy).reshape(n_gx, GRAIN_DEV, NZ)
    got_rows = lax.all_to_all(rows, "gx", split_axis=0, concat_axis=0, tiled=True)
    (base,) = local_step(costate, fields_zero, False)
    (adjoint,) = fix(place, costate, fields_zero, got_faces, got_sides, base)
    grain_grad = jnp.sum(got_rows.reshape(n_gx, GRAIN_DEV, NZ), axis=0)
    return adjoint, grain_grad


def solution(mesh):
    placed = (
        P(None, "gx", "gy", None),
        P(None, "gx", "gy", None),
        P(None, "gx", "gy", None),
        P("gx", "gy", None),
    )
    return jax.shard_map(
        functools.partial(shards, mesh.shape["gx"], mesh.shape["gy"]),
        mesh=mesh,
        in_specs=placed,
        out_specs=(P(None, "gx", "gy", None), P(("gx", "gy"), None)),
        check_vma=False,
    )
```

```python
import functools

import jax
import jax.numpy as jnp
from jax import lax
from jax.experimental import pallas as pl
from jax.experimental.pallas import tpu as pltpu
from jax.sharding import PartitionSpec as P

DT = 0.05
SLOTS = 8
NF = SLOTS + 1
CX, CY, NZ = 8, 64, 256
LN = 128
HALF = NZ // LN
GRAIN_DEV = 8
PAD = 8
ROWS = CY + 2 * PAD
FACE = (SLOTS + 2) * CY
FACE_ROWS = FACE + 8
SIDE_ROWS = (SLOTS + 2) * CX
F32 = jnp.float32
BOTH = range(HALF)
LIMIT = 4 << 20
HBM = pl.BlockSpec(memory_space=pltpu.HBM)
VM = pl.BlockSpec(memory_space=pltpu.VMEM)
SM = pl.BlockSpec(memory_space=pltpu.SMEM)


def lanes(half):
    return slice(half * LN, (half + 1) * LN)


def z_sum(first, second):
    lane = lax.broadcasted_iota(jnp.int32, first.shape, first.ndim - 1)
    axis = first.ndim - 1
    low, high = lane == 0, lane == LN - 1
    from_low = pltpu.roll(first, 1, axis)
    from_high = pltpu.roll(second, LN - 1, axis)
    left = jnp.where(low, 0.0, from_low), jnp.where(low, from_low, pltpu.roll(second, 1, axis))
    right = jnp.where(high, from_high, pltpu.roll(first, LN - 1, axis)), jnp.where(high, 0.0, from_high)
    return left[0] + right[0], left[1] + right[1]


def start_all(copies):
    for copy in copies:
        copy.start()
    return copies


def wait_all(copies):
    for copy in copies:
        copy.wait()


def around(ref, x, row):
    own = [ref[h, x + 1, row : row + 8, :] for h in BOTH]
    along_z = z_sum(*own)
    total = [
        (ref[h, x, row : row + 8, :] + ref[h, x + 2, row : row + 8, :])
        + (ref[h, x + 1, row - 1 : row + 7, :] + ref[h, x + 1, row + 1 : row + 9, :])
        + along_z[h]
        for h in BOTH
    ]
    return own, total


def clear_edges(ref):
    tile = jnp.zeros((8, LN), F32)
    plane = jnp.zeros((CY, LN), F32)
    for h in BOTH:
        ref[h, 0, PAD : PAD + CY, :] = plane
        ref[h, CX + 1, PAD : PAD + CY, :] = plane
        for x in range(1, CX + 1):
            ref[h, x, 0:PAD, :] = tile
            ref[h, x, PAD + CY : ROWS, :] = tile


def local_kernel(with_sums, cos, fld, out, density_value, field, result, *rest):
    if with_sums:
        sums, *rest = rest
    phases, potential, sem_c, sem_e, sem_f, sem_o, sem_d = rest

    def copy_c(h):
        return pltpu.make_async_copy(
            cos.at[0, :, :, lanes(h)],
            density_value.at[h, 1 : CX + 1, PAD : PAD + CY, :],
            sem_c.at[h],
        )

    def copy_e(x, h):
        return pltpu.make_async_copy(
            cos.at[1:NF, x, :, lanes(h)], phases.at[:, h, x + 1, PAD : PAD + CY, :], sem_e.at[x, h]
        )

    def copy_f(x, h):
        return pltpu.make_async_copy(fld.at[:, x, :, lanes(h)], field.at[:, h, x], sem_f.at[x, h])

    inside = slice(8, CY - 8)

    def copy_o(x, h):
        return pltpu.make_async_copy(
            result.at[1:NF, h, x, inside, :], out.at[1:NF, x, inside, lanes(h)], sem_o.at[x, h]
        )

    def copy_d(x, h):
        return pltpu.make_async_copy(
            result.at[0, h, x, inside, :], out.at[0, x, inside, lanes(h)], sem_d.at[x, h]
        )

    for h in BOTH:
        copy_c(h).start()
    for x in range(CX):
        for h in BOTH:
            copy_e(x, h).start()
            copy_f(x, h).start()

    clear_edges(potential)
    clear_edges(density_value)
    for s in range(SLOTS):
        clear_edges(phases.at[s])
    if with_sums:
        sums[...] = jnp.zeros(sums.shape, F32)
    for h in BOTH:
        copy_c(h).wait()

    def potential_plane(x, carry):
        for part in range(CY // 8):
            row = PAD + part * 8
            own, total = around(density_value, x, row)
            for h in BOTH:
                potential[h, x + 1, row : row + 8, :] = DT * total[h] - (6.0 * DT) * own[h]
        return carry

    lax.fori_loop(0, CX, potential_plane, 0)

    for h in BOTH:
        copy_e(0, h).wait()

    def step_plane(x, carry):
        @pl.when(x < CX - 1)
        def _():
            for h in BOTH:
                copy_e(x + 1, h).wait()

        for h in BOTH:
            copy_f(x, h).wait()
        for part in range(CY // 8):
            row = PAD + part * 8
            here = slice(part * 8, part * 8 + 8)
            square = [None] * HALF
            weighted = [None] * HALF
            curved = [None] * HALF
            for s in range(SLOTS):
                for h in BOTH:
                    eta = field[s + 1, h, x, here, :]
                    lam = phases[s, h, x + 1, row : row + 8, :]
                    eta_eta = eta * eta
                    lam_eta = lam * eta
                    cubic = lam_eta * eta
                    square[h] = eta_eta if square[h] is None else square[h] + eta_eta
                    weighted[h] = lam_eta if weighted[h] is None else weighted[h] + lam_eta
                    curved[h] = cubic if curved[h] is None else curved[h] + cubic
            mu, mu_total = around(potential, x, row)
            scale, slope, mu_twelve, linear = [], [], [], []
            for h in BOTH:
                density = field[0, h, x, here, :]
                lam_c = density_value[h, x + 1, row : row + 8, :]
                curvature = 34.0 + density * (192.0 * density - 192.0)
                result[0, h, x, here, :] = (
                    lam_c
                    + mu[h] * (curvature + 6.0)
                    - mu_total[h]
                    - (12.0 * DT) * (curved[h] - weighted[h])
                )
                scale.append((1.0 - 18.0 * DT) + (12.0 * DT) * (density - square[h]))
                slope.append((48.0 * DT) - (24.0 * DT) * density)
                mu_twelve.append(12.0 * mu[h])
                linear.append((24.0 * DT) * weighted[h] + mu_twelve[h])
            for s in range(SLOTS):
                lam, total = around(phases.at[s], x, row)
                for h in BOTH:
                    eta = field[s + 1, h, x, here, :]
                    new = (
                        lam[h] * (scale[h] + slope[h] * eta)
                        + eta * (mu_twelve[h] * eta - linear[h])
                        + DT * total[h]
                    )
                    result[s + 1, h, x, here, :] = new
                    if with_sums:
                        sums[s, h, here, :] += lam[h] + new

        @pl.when((x > 0) & (x < CX - 1))
        def _():
            for h in BOTH:
                copy_o(x, h).start()

        @pl.when((x > 1) & (x < CX - 2))
        def _():
            for h in BOTH:
                copy_d(x, h).start()

        return carry

    lax.fori_loop(0, CX, step_plane, 0)
    for h in BOTH:
        for x in range(1, CX - 1):
            copy_o(x, h).wait()
        for x in range(2, CX - 2):
            copy_d(x, h).wait()


PADDED = jax.ShapeDtypeStruct((HALF, CX + 2, ROWS, LN), F32)
BLOCK = jax.ShapeDtypeStruct((NF, HALF, CX, CY, LN), F32)
SUMS = jax.ShapeDtypeStruct((SLOTS, HALF, CY, LN), F32)
WHOLE = pltpu.HBM((NF, CX, CY, NZ), F32)


def local_step(cos, fld, with_sums):
    extra = [SUMS] if with_sums else []
    return pl.pallas_call(
        functools.partial(local_kernel, with_sums),
        out_shape=[WHOLE, PADDED, BLOCK, BLOCK] + extra,
        in_specs=[HBM, HBM],
        out_specs=[HBM, VM, VM, VM] + [VM] * len(extra),
        scratch_shapes=[
            pltpu.VMEM((SLOTS, HALF, CX + 2, ROWS, LN), F32),
            pltpu.VMEM((HALF, CX + 2, ROWS, LN), F32),
            pltpu.SemaphoreType.DMA((HALF,)),
            pltpu.SemaphoreType.DMA((CX, HALF)),
            pltpu.SemaphoreType.DMA((CX, HALF)),
            pltpu.SemaphoreType.DMA((CX, HALF)),
            pltpu.SemaphoreType.DMA((CX, HALF)),
        ],
        compiler_params=pltpu.CompilerParams(vmem_limit_bytes=12 << 20),
        cost_estimate=pl.CostEstimate(
            flops=250 * CX * CY * NZ, bytes_accessed=3 * 4 * NF * CX * CY * NZ, transcendentals=0
        ),
        name="local_step",
    )(cos, fld)


def pack_kernel(place, cos, face_a, face_b, side_a, side_b, tiles, sem_p, sem_t):
    even_x = place[0] == 0
    even_y = place[1] == 0
    out_a = jnp.where(even_x, CX - 1, 0)
    in_a = jnp.where(even_x, CX - 2, 1)
    loads = start_all(
        [
            pltpu.make_async_copy(
                cos.at[:, :, edge * (CY - 8) : edge * (CY - 8) + 8, :], tiles.at[edge], sem_t.at[edge]
            )
            for edge in range(2)
        ]
    )
    copies = []
    for which, face, outer, inner in ((0, face_a, out_a, in_a), (1, face_b, CX - 1 - out_a, CX - 1 - in_a)):
        for h in range(HALF):
            for k in range(SLOTS + 2):
                s = k + 1 if k < SLOTS else 0
                x = inner if k == SLOTS + 1 else outer
                copies.append(
                    pltpu.make_async_copy(
                        cos.at[s, x, :, lanes(h)],
                        face.at[h, k * CY : (k + 1) * CY, :],
                        sem_p.at[which, h, k],
                    )
                )
    start_all(copies)
    wait_all(loads)
    for h in range(HALF):
        for k in range(SLOTS + 2):
            s = k + 1 if k < SLOTS else 0
            depth = 1 if k == SLOTS + 1 else 0
            low = tiles[0, s, :, depth, lanes(h)]
            high = tiles[1, s, :, 7 - depth, lanes(h)]
            side_a[h, k * CX : (k + 1) * CX, :] = jnp.where(even_y, high, low)
            side_b[h, k * CX : (k + 1) * CX, :] = jnp.where(even_y, low, high)
    wait_all(copies)


def pack(place, cos):
    face = jax.ShapeDtypeStruct((HALF, FACE_ROWS, LN), F32)
    side = jax.ShapeDtypeStruct((HALF, SIDE_ROWS, LN), F32)
    return pl.pallas_call(
        pack_kernel,
        out_shape=[face, face, side, side],
        in_specs=[SM, HBM],
        out_specs=[VM] * 4,
        scratch_shapes=[
            pltpu.VMEM((2, NF, CX, 8, NZ), F32),
            pltpu.SemaphoreType.DMA((2, HALF, SLOTS + 2)),
            pltpu.SemaphoreType.DMA((2,)),
        ],
        compiler_params=pltpu.CompilerParams(vmem_limit_bytes=8 << 20),
        name="pack",
    )(place, cos)


def corner_kernel(place, got_a, got_b, face_a, face_b, out_a, out_b):
    del face_a, face_b
    even_x = place[0] == 0
    even_y = place[1] == 0
    row = lax.broadcasted_iota(jnp.int32, (8, LN), 0)
    for h in BOTH:
        here = slice(SLOTS * CX, SLOTS * CX + CX)
        first, second = got_a[h, here, :], got_b[h, here, :]
        low = jnp.where(even_y, second, first)
        high = jnp.where(even_y, first, second)
        at_low = jnp.where(row == 0, low[0:1, :], high[0:1, :])
        at_high = jnp.where(row == 0, low[CX - 1 : CX, :], high[CX - 1 : CX, :])
        out_a[h, FACE:FACE_ROWS, :] = jnp.where(even_x, at_high, at_low)
        out_b[h, FACE:FACE_ROWS, :] = jnp.where(even_x, at_low, at_high)


FACE_MESSAGE = jax.ShapeDtypeStruct((HALF, FACE_ROWS, LN), F32)
SIDE_MESSAGE = jax.ShapeDtypeStruct((HALF, SIDE_ROWS, LN), F32)


def corner(place, got, faces):
    return pl.pallas_call(
        corner_kernel,
        out_shape=[FACE_MESSAGE] * 2,
        in_specs=[SM] + [VM] * 4,
        out_specs=[VM] * 2,
        input_output_aliases={3: 0, 4: 1},
        compiler_params=pltpu.CompilerParams(vmem_limit_bytes=LIMIT),
        name="corner",
    )(place, *got, *faces)


def fix_kernel(first_step, place, value, field, got_fa, got_fb, got_sa, got_sb, *rest):
    if first_step:
        _, _, _, work, out, sums, face_a, face_b, side_a, side_b, edge, sem = rest
    else:
        _, _, work, out, edge, sem = rest
    even_x = place[0] == 0
    even_y = place[1] == 0
    stores = []

    def store(*where):
        s, x, y = where
        for h in BOTH:
            stores.append(
                pltpu.make_async_copy(work.at[s, h, x, y, :], out.at[s, x, y, lanes(h)], sem.at[len(stores)])
            )
            stores[-1].start()

    row = lax.broadcasted_iota(jnp.int32, (CX, LN), 0)
    for y, inner, present in ((0, 1, place[4]), (CY - 1, CY - 2, place[5])):

        def got(h, start):
            a = got_sa[h, start : start + CX, :]
            b = got_sb[h, start : start + CX, :]
            return jnp.where(even_y, b, a) if y == 0 else jnp.where(even_y, a, b)

        exists = present.astype(F32) * DT
        delta = [DT * got(h, SLOTS * CX) for h in BOTH]
        along_z = z_sum(*delta)
        twelve = []
        for h in BOTH:
            d = delta[h]
            along_x = jnp.where(row == 0, 0.0, pltpu.roll(d, 1, 0)) + jnp.where(
                row == CX - 1, 0.0, pltpu.roll(d, CX - 1, 0)
            )
            total = along_z[h] + along_x - 6.0 * d
            density = field[0, h, :, y, :]
            curvature = 34.0 + density * (192.0 * density - 192.0)
            work[0, h, :, y, :] = work[0, h, :, y, :] + (
                d * curvature
                - 2.0 * total
                - DT * got(h, (SLOTS + 1) * CX)
                - exists * value[h, 1 : CX + 1, PAD + y, :]
            )
            work[0, h, :, inner, :] = work[0, h, :, inner, :] - d
            twelve.append(12.0 * d)
        for s in range(1, NF):
            for h in BOTH:
                eta = field[s, h, :, y, :]
                change = DT * got(h, (s - 1) * CX) + twelve[h] * (eta * eta - eta)
                work[s, h, :, y, :] = work[s, h, :, y, :] + change
                if first_step:
                    sums[s - 1, h, y : y + 1, :] += jnp.sum(change, axis=0, keepdims=True)
        near = slice(0, 8) if y == 0 else slice(CY - 8, CY)
        store(slice(1, NF), slice(1, CX - 1), near)
        store(0, slice(2, CX - 2), near)

    for x, inner, present in ((0, 1, place[2]), (CX - 1, CX - 2, place[3])):

        def got(h, start, size):
            a = got_fa[h, start : start + size, :]
            b = got_fb[h, start : start + size, :]
            return jnp.where(even_x, b, a) if x == 0 else jnp.where(even_x, a, b)

        exists = present.astype(F32) * DT
        delta = []
        for h in BOTH:
            d = DT * got(h, SLOTS * CY, CY)
            ends = DT * got(h, FACE, 8)
            delta.append(d)
            edge[h, 8 : 8 + CY, :] = d
            edge[h, 7:8, :] = ends[0:1, :]
            edge[h, 8 + CY : 9 + CY, :] = ends[1:2, :]
        along_z = z_sum(*delta)
        twelve = []
        for h in BOTH:
            total = along_z[h] + edge[h, 9 : 9 + CY, :] + edge[h, 7 : 7 + CY, :] - 6.0 * delta[h]
            density = field[0, h, x]
            curvature = 34.0 + density * (192.0 * density - 192.0)
            work[0, h, x] += (
                delta[h] * curvature
                - 2.0 * total
                - DT * got(h, (SLOTS + 1) * CY, CY)
                - exists * value[h, x + 1, PAD : PAD + CY, :]
            )
            work[0, h, inner] -= delta[h]
            twelve.append(12.0 * delta[h])
        for s in range(1, NF):
            for h in BOTH:
                eta = field[s, h, x]
                change = DT * got(h, (s - 1) * CY, CY) + twelve[h] * (eta * eta - eta)
                work[s, h, x] += change
                if first_step:
                    sums[s - 1, h] += change
        store(slice(0, NF), x, slice(0, CY))
        store(0, inner, slice(0, CY))

    if first_step:
        for h in BOTH:
            for k in range(SLOTS + 2):
                s = k + 1 if k < SLOTS else 0
                depth = 1 if k == SLOTS + 1 else 0
                low, high = (work[s, h, x] for x in (depth, CX - 1 - depth))
                face_a[h, k * CY : (k + 1) * CY, :] = jnp.where(even_x, high, low)
                face_b[h, k * CY : (k + 1) * CY, :] = jnp.where(even_x, low, high)
                low, high = (work[s, h, :, y, :] for y in (depth, CY - 1 - depth))
                side_a[h, k * CX : (k + 1) * CX, :] = jnp.where(even_y, high, low)
                side_b[h, k * CX : (k + 1) * CX, :] = jnp.where(even_y, low, high)
    wait_all(stores)


def fix(place, value, field, got_faces, got_sides, base, out, sums=None):
    first_step = sums is not None
    args = [place, value, field, *got_faces, *got_sides, base, out]
    in_specs = [SM] + [VM] * 7 + [HBM]
    out_shape, out_specs = [BLOCK, WHOLE], [VM, HBM]
    aliases = {7: 0, 8: 1}
    if first_step:
        args.append(sums)
        in_specs.append(VM)
        out_shape += [SUMS] + [FACE_MESSAGE] * 2 + [SIDE_MESSAGE] * 2
        out_specs += [VM] * 5
        aliases[9] = 2
    return pl.pallas_call(
        functools.partial(fix_kernel, first_step),
        out_shape=out_shape,
        in_specs=in_specs,
        out_specs=out_specs,
        scratch_shapes=[pltpu.VMEM((HALF, ROWS, LN), F32), pltpu.SemaphoreType.DMA((16,))],
        input_output_aliases=aliases,
        compiler_params=pltpu.CompilerParams(vmem_limit_bytes=LIMIT),
        name="fix",
    )(*args)[1:]


def grain_kernel(groups, grains, sums, rows):
    rows[...] = jnp.zeros(rows.shape, F32)
    row = lax.broadcasted_iota(jnp.int32, (GRAIN_DEV, LN), 0)
    for t in range(CY // 8):
        for s in range(SLOTS):
            grain = grains[0, t, s]
            start = pl.multiple_of(grain // (GRAIN_DEV * groups) * GRAIN_DEV, GRAIN_DEV)
            chosen = row == grain % GRAIN_DEV
            for h in range(HALF):
                total = DT * jnp.sum(sums[s, h, t * 8 : t * 8 + 8, :], axis=0, keepdims=True)
                rows[pl.ds(start, GRAIN_DEV), lanes(h)] += jnp.where(chosen, total, 0.0)


def grain_rows(slot_grain, sums, peers, groups):
    return pl.pallas_call(
        functools.partial(grain_kernel, groups),
        out_shape=jax.ShapeDtypeStruct((peers * GRAIN_DEV, NZ), F32),
        in_specs=[SM, VM],
        out_specs=VM,
        compiler_params=pltpu.CompilerParams(vmem_limit_bytes=LIMIT),
        name="grain_rows",
    )(slot_grain, sums)


def swaps(axis, count, first, second):
    near = [(i, i ^ 1) for i in range(count)]
    far = [(i, ((i + 1) ^ 1) - 1) for i in range(1, count - 1)]
    return lax.ppermute(first, axis, near), lax.ppermute(second, axis, far)


def shards(n_gx, n_gy, cotangent, fields_one, fields_zero, slot_grain):
    gx, gy = lax.axis_index("gx"), lax.axis_index("gy")
    cotangent, fields_one, fields_zero = (
        pltpu.with_memory_space_constraint(array, pltpu.HBM)
        for array in (cotangent, fields_one, fields_zero)
    )
    place = jnp.stack(
        [gx % 2, gy % 2, gx > 0, gx < n_gx - 1, gy > 0, gy < n_gy - 1]
    ).astype(jnp.int32)

    def exchange(faces, sides):
        got_sides = swaps("gy", n_gy, *sides)
        faces = corner(place, got_sides, faces)
        return swaps("gx", n_gx, *faces), got_sides

    face_a, face_b, side_a, side_b = pack(place, cotangent)
    got_faces, got_sides = exchange((face_a, face_b), (side_a, side_b))
    out, value, field, base, sums = local_step(cotangent, fields_one, True)
    costate, sums, face_a, face_b, side_a, side_b = fix(
        place, value, field, got_faces, got_sides, base, out, sums
    )

    got_faces, got_sides = exchange((face_a, face_b), (side_a, side_b))
    rows = grain_rows(slot_grain, sums, n_gx, n_gy).reshape(n_gx, GRAIN_DEV, NZ)
    got_rows = lax.all_to_all(rows, "gx", split_axis=0, concat_axis=0, tiled=True)
    costate = pltpu.with_memory_space_constraint(costate, pltpu.HBM)
    out, value, field, base = local_step(costate, fields_zero, False)
    (adjoint,) = fix(place, value, field, got_faces, got_sides, base, out)
    got_rows, adjoint = lax.optimization_barrier((got_rows, adjoint))
    grain_grad = jnp.sum(got_rows.reshape(n_gx, GRAIN_DEV, NZ), axis=0)
    return adjoint, grain_grad


def solution(mesh):
    placed = (
        P(None, "gx", "gy", None),
        P(None, "gx", "gy", None),
        P(None, "gx", "gy", None),
        P("gx", "gy", None),
    )
    return jax.shard_map(
        functools.partial(shards, mesh.shape["gx"], mesh.shape["gy"]),
        mesh=mesh,
        in_specs=placed,
        out_specs=(P(None, "gx", "gy", None), P(("gx", "gy"), None)),
        check_vma=False,
    )
```

```python
import functools

import jax
import jax.numpy as jnp
from jax import lax
from jax.experimental import pallas as pl
from jax.experimental.pallas import tpu as pltpu
from jax.sharding import PartitionSpec as P

DT = 0.05
SLOTS = 8
NF = SLOTS + 1
CX, CY, NZ = 8, 64, 256
LN = 128
HALF = NZ // LN
GRAIN_DEV = 8
PAD = 8
ROWS = CY + 2 * PAD
FACE = (SLOTS + 2) * CY
SIDE = (SLOTS + 2) * CX
EXTRA = 8
F32 = jnp.float32
BOTH = range(HALF)
LIMIT = 4 << 20
HBM = pl.BlockSpec(memory_space=pltpu.HBM)
VM = pl.BlockSpec(memory_space=pltpu.VMEM)
SM = pl.BlockSpec(memory_space=pltpu.SMEM)


def lanes(half):
    return slice(half * LN, (half + 1) * LN)


def z_sum(first, second):
    lane = lax.broadcasted_iota(jnp.int32, first.shape, first.ndim - 1)
    axis = first.ndim - 1
    low, high = lane == 0, lane == LN - 1
    from_low = pltpu.roll(first, 1, axis)
    from_high = pltpu.roll(second, LN - 1, axis)
    left = jnp.where(low, 0.0, from_low), jnp.where(low, from_low, pltpu.roll(second, 1, axis))
    right = jnp.where(high, from_high, pltpu.roll(first, LN - 1, axis)), jnp.where(high, 0.0, from_high)
    return left[0] + right[0], left[1] + right[1]


def start_all(copies):
    for copy in copies:
        copy.start()
    return copies


def wait_all(copies):
    for copy in copies:
        copy.wait()


def around(ref, x, row):
    own = [ref[h, x + 1, row : row + 8, :] for h in BOTH]
    along_z = z_sum(*own)
    total = [
        (ref[h, x, row : row + 8, :] + ref[h, x + 2, row : row + 8, :])
        + (ref[h, x + 1, row - 1 : row + 7, :] + ref[h, x + 1, row + 1 : row + 9, :])
        + along_z[h]
        for h in BOTH
    ]
    return own, total


def clear_edges(ref):
    tile = jnp.zeros((8, LN), F32)
    plane = jnp.zeros((CY, LN), F32)
    for h in BOTH:
        ref[h, 0, PAD : PAD + CY, :] = plane
        ref[h, CX + 1, PAD : PAD + CY, :] = plane
        for x in range(1, CX + 1):
            ref[h, x, 0:PAD, :] = tile
            ref[h, x, PAD + CY : ROWS, :] = tile


def local_kernel(with_sums, cos, fld, *rest):
    if with_sums:
        out, density_value, field, result, sums, *rest = rest
    else:
        corners, out, density_value, field, result, *rest = rest
    phases, potential, sem_c, sem_e, sem_f, sem_o, sem_d = rest

    def copy_c(h):
        return pltpu.make_async_copy(
            cos.at[0, :, :, lanes(h)],
            density_value.at[h, 1 : CX + 1, PAD : PAD + CY, :],
            sem_c.at[h],
        )

    def copy_e(x, h):
        return pltpu.make_async_copy(
            cos.at[1:NF, x, :, lanes(h)], phases.at[:, h, x + 1, PAD : PAD + CY, :], sem_e.at[x, h]
        )

    def copy_f(x, h):
        return pltpu.make_async_copy(fld.at[:, x, :, lanes(h)], field.at[:, h, x], sem_f.at[x, h])

    inside = slice(8, CY - 8)

    def copy_o(x, h):
        return pltpu.make_async_copy(
            result.at[1:NF, h, x, inside, :], out.at[1:NF, x, inside, lanes(h)], sem_o.at[x, h]
        )

    def copy_d(x, h):
        return pltpu.make_async_copy(
            result.at[0, h, x, inside, :], out.at[0, x, inside, lanes(h)], sem_d.at[x, h]
        )

    for h in BOTH:
        copy_c(h).start()
    for x in range(CX):
        for h in BOTH:
            copy_e(x, h).start()
            copy_f(x, h).start()

    clear_edges(potential)
    clear_edges(density_value)
    for s in range(SLOTS):
        clear_edges(phases.at[s])
    if with_sums:
        sums[...] = jnp.zeros(sums.shape, F32)
    for h in BOTH:
        copy_c(h).wait()
        if not with_sums:
            for edge, y in ((0, PAD), (8, PAD + CY - 1)):
                for k, x in ((0, 1), (1, CX)):
                    density_value[h, x, y : y + 1, :] += corners[h, edge + k : edge + k + 1, :]

    def potential_plane(x, carry):
        for part in range(CY // 8):
            row = PAD + part * 8
            own, total = around(density_value, x, row)
            for h in BOTH:
                potential[h, x + 1, row : row + 8, :] = DT * total[h] - (6.0 * DT) * own[h]
        return carry

    lax.fori_loop(0, CX, potential_plane, 0)

    for h in BOTH:
        copy_e(0, h).wait()

    def step_plane(x, carry):
        @pl.when(x < CX - 1)
        def _():
            for h in BOTH:
                copy_e(x + 1, h).wait()

        for h in BOTH:
            copy_f(x, h).wait()
        for part in range(CY // 8):
            row = PAD + part * 8
            here = slice(part * 8, part * 8 + 8)
            square = [None] * HALF
            weighted = [None] * HALF
            curved = [None] * HALF
            for s in range(SLOTS):
                for h in BOTH:
                    eta = field[s + 1, h, x, here, :]
                    lam = phases[s, h, x + 1, row : row + 8, :]
                    eta_eta = eta * eta
                    lam_eta = lam * eta
                    cubic = lam_eta * eta
                    square[h] = eta_eta if square[h] is None else square[h] + eta_eta
                    weighted[h] = lam_eta if weighted[h] is None else weighted[h] + lam_eta
                    curved[h] = cubic if curved[h] is None else curved[h] + cubic
            mu, mu_total = around(potential, x, row)
            scale, slope, mu_twelve, linear = [], [], [], []
            for h in BOTH:
                density = field[0, h, x, here, :]
                lam_c = density_value[h, x + 1, row : row + 8, :]
                curvature = 34.0 + density * (192.0 * density - 192.0)
                result[0, h, x, here, :] = (
                    lam_c
                    + mu[h] * (curvature + 6.0)
                    - mu_total[h]
                    - (12.0 * DT) * (curved[h] - weighted[h])
                )
                scale.append((1.0 - 18.0 * DT) + (12.0 * DT) * (density - square[h]))
                slope.append((48.0 * DT) - (24.0 * DT) * density)
                mu_twelve.append(12.0 * mu[h])
                linear.append((24.0 * DT) * weighted[h] + mu_twelve[h])
            for s in range(SLOTS):
                lam, total = around(phases.at[s], x, row)
                for h in BOTH:
                    eta = field[s + 1, h, x, here, :]
                    new = (
                        lam[h] * (scale[h] + slope[h] * eta)
                        + eta * (mu_twelve[h] * eta - linear[h])
                        + DT * total[h]
                    )
                    result[s + 1, h, x, here, :] = new
                    if with_sums:
                        sums[s, h, here, :] += lam[h] + new

        @pl.when((x > 0) & (x < CX - 1))
        def _():
            for h in BOTH:
                copy_o(x, h).start()

        @pl.when((x > 1) & (x < CX - 2))
        def _():
            for h in BOTH:
                copy_d(x, h).start()

        return carry

    lax.fori_loop(0, CX, step_plane, 0)
    for h in BOTH:
        for x in range(1, CX - 1):
            copy_o(x, h).wait()
        for x in range(2, CX - 2):
            copy_d(x, h).wait()


PADDED = jax.ShapeDtypeStruct((HALF, CX + 2, ROWS, LN), F32)
BLOCK = jax.ShapeDtypeStruct((NF, HALF, CX, CY, LN), F32)
SUMS = jax.ShapeDtypeStruct((SLOTS, HALF, CY, LN), F32)
WHOLE = pltpu.HBM((NF, CX, CY, NZ), F32)


def local_step(cos, fld, corners=None):
    with_sums = corners is None
    extra = [SUMS] if with_sums else []
    more = [] if with_sums else [corners]
    return pl.pallas_call(
        functools.partial(local_kernel, with_sums),
        out_shape=[WHOLE, PADDED, BLOCK, BLOCK] + extra,
        in_specs=[HBM, HBM] + [VM] * len(more),
        out_specs=[HBM, VM, VM, VM] + [VM] * len(extra),
        scratch_shapes=[
            pltpu.VMEM((SLOTS, HALF, CX + 2, ROWS, LN), F32),
            pltpu.VMEM((HALF, CX + 2, ROWS, LN), F32),
            pltpu.SemaphoreType.DMA((HALF,)),
            pltpu.SemaphoreType.DMA((CX, HALF)),
            pltpu.SemaphoreType.DMA((CX, HALF)),
            pltpu.SemaphoreType.DMA((CX, HALF)),
            pltpu.SemaphoreType.DMA((CX, HALF)),
        ],
        compiler_params=pltpu.CompilerParams(vmem_limit_bytes=12 << 20),
        cost_estimate=pl.CostEstimate(
            flops=250 * CX * CY * NZ, bytes_accessed=3 * 4 * NF * CX * CY * NZ, transcendentals=0
        ),
        name="local_step",
    )(cos, fld, *more)


def pack_kernel(place, cos, face_a, face_b, side_a, side_b, tiles, sem_p, sem_t):
    even_x = place[0] == 0
    even_y = place[1] == 0
    out_a = jnp.where(even_x, CX - 1, 0)
    in_a = jnp.where(even_x, CX - 2, 1)
    loads = start_all(
        [
            pltpu.make_async_copy(
                cos.at[:, :, edge * (CY - 8) : edge * (CY - 8) + 8, :], tiles.at[edge], sem_t.at[edge]
            )
            for edge in range(2)
        ]
    )
    copies = []
    for which, face, outer, inner in ((0, face_a, out_a, in_a), (1, face_b, CX - 1 - out_a, CX - 1 - in_a)):
        for h in BOTH:
            phases = face.at[h, 0 : SLOTS * CY, :].reshape(SLOTS, CY, LN)
            parts = (
                (cos.at[1:NF, outer, :, lanes(h)], phases),
                (cos.at[0, outer, :, lanes(h)], face.at[h, SLOTS * CY : SLOTS * CY + CY, :]),
                (cos.at[0, inner, :, lanes(h)], face.at[h, SLOTS * CY + CY : FACE, :]),
            )
            copies += [
                pltpu.make_async_copy(*part, sem_p.at[which, h, k]) for k, part in enumerate(parts)
            ]
    start_all(copies)
    wait_all(loads)
    for h in range(HALF):
        for k in range(SLOTS + 2):
            s = k + 1 if k < SLOTS else 0
            depth = 1 if k == SLOTS + 1 else 0
            low = tiles[0, s, :, depth, lanes(h)]
            high = tiles[1, s, :, 7 - depth, lanes(h)]
            side_a[h, k * CX : (k + 1) * CX, :] = jnp.where(even_y, high, low)
            side_b[h, k * CX : (k + 1) * CX, :] = jnp.where(even_y, low, high)
    wait_all(copies)


def face_message(extra):
    return jax.ShapeDtypeStruct((HALF, FACE + extra, LN), F32)


def side_message(extra):
    return jax.ShapeDtypeStruct((HALF, SIDE + extra, LN), F32)


def pack(place, cos):
    return pl.pallas_call(
        pack_kernel,
        out_shape=[face_message(0)] * 2 + [side_message(0)] * 2,
        in_specs=[SM, HBM],
        out_specs=[VM] * 4,
        scratch_shapes=[
            pltpu.VMEM((2, NF, CX, 8, NZ), F32),
            pltpu.SemaphoreType.DMA((2, HALF, 3)),
            pltpu.SemaphoreType.DMA((2,)),
        ],
        compiler_params=pltpu.CompilerParams(vmem_limit_bytes=8 << 20),
        name="pack",
    )(place, cos)


def corner_kernel(place, first_a, first_b, order, got_a, got_b, face_a, face_b, *rest):
    del order, got_a, got_b, face_a, face_b
    side_a, side_b, out_a, out_b, corners = rest
    even_x = place[0] == 0
    even_y = place[1] == 0
    row = lax.broadcasted_iota(jnp.int32, (CX, LN), 0)
    face = slice(SLOTS * CX, SLOTS * CX + CX)
    start = SLOTS * CY
    for h in BOTH:
        ends_a = first_a[h, start : start + 1, :], first_a[h, start + CY - 1 : start + CY, :]
        ends_b = first_b[h, start : start + 1, :], first_b[h, start + CY - 1 : start + CY, :]
        fixed = []
        for ref, low_side in ((side_a, ~even_y), (side_b, even_y)):
            end_a = jnp.where(low_side, ends_a[0], ends_a[1])
            end_b = jnp.where(low_side, ends_b[0], ends_b[1])
            at_low = jnp.where(even_x, end_b, end_a)
            at_high = jnp.where(even_x, end_a, end_b)
            term = jnp.where(row == 0, at_low, jnp.where(row == CX - 1, at_high, 0.0))
            exists = jnp.where(low_side, place[4], place[5]).astype(F32)
            value = ref[h, face, :] - (2.0 * DT * exists) * term
            ref[h, face, :] = value
            fixed.append(value)
        low = jnp.where(even_y, fixed[1], fixed[0])
        high = jnp.where(even_y, fixed[0], fixed[1])
        beyond_a, beyond_b = side_a[h, SIDE : SIDE + 8, :], side_b[h, SIDE : SIDE + 8, :]
        beyond_low = (-2.0 * DT) * jnp.where(even_y, beyond_b, beyond_a)
        beyond_high = (-2.0 * DT) * jnp.where(even_y, beyond_a, beyond_b)
        corners[h, 0:8, :] = beyond_low
        corners[h, 8:16, :] = beyond_high
        at_low = jnp.where(row == 0, low[0:1, :], high[0:1, :])
        at_high = jnp.where(row == 0, low[CX - 1 : CX, :], high[CX - 1 : CX, :])
        for ref, high_face in ((out_a, even_x), (out_b, ~even_x)):
            ref[h, FACE : FACE + 8, :] = jnp.where(high_face, at_high, at_low)
            ref[h, start : start + 1, :] += jnp.where(high_face, beyond_low[1:2, :], beyond_low[0:1, :])
            ref[h, start + CY - 1 : start + CY, :] += jnp.where(
                high_face, beyond_high[1:2, :], beyond_high[0:1, :]
            )


CORNERS = jax.ShapeDtypeStruct((HALF, 16, LN), F32)


def corner(place, first, order, got, faces):
    return pl.pallas_call(
        corner_kernel,
        out_shape=[side_message(EXTRA)] * 2 + [face_message(EXTRA)] * 2 + [CORNERS],
        in_specs=[SM, VM, VM, HBM] + [VM] * 4,
        out_specs=[VM] * 5,
        input_output_aliases={4: 0, 5: 1, 6: 2, 7: 3},
        compiler_params=pltpu.CompilerParams(vmem_limit_bytes=LIMIT),
        name="corner",
    )(place, *first, order, *got, *faces)


def fix_kernel(first_step, place, value, field, got_fa, got_fb, got_sa, got_sb, *rest):
    if first_step:
        _, _, _, work, out, sums, face_a, face_b, side_a, side_b, edge, sem = rest
    else:
        _, _, work, out, edge, sem = rest
    even_x = place[0] == 0
    even_y = place[1] == 0
    stores = []

    def store(*where):
        s, x, y = where
        for h in BOTH:
            stores.append(
                pltpu.make_async_copy(work.at[s, h, x, y, :], out.at[s, x, y, lanes(h)], sem.at[len(stores)])
            )
            stores[-1].start()

    row = lax.broadcasted_iota(jnp.int32, (CX, LN), 0)
    for y, inner, present in ((0, 1, place[4]), (CY - 1, CY - 2, place[5])):

        def got(h, start):
            a = got_sa[h, start : start + CX, :]
            b = got_sb[h, start : start + CX, :]
            return jnp.where(even_y, b, a) if y == 0 else jnp.where(even_y, a, b)

        exists = present.astype(F32) * DT
        delta = [DT * got(h, SLOTS * CX) for h in BOTH]
        along_z = z_sum(*delta)
        twelve = []
        for h in BOTH:
            d = delta[h]
            along_x = jnp.where(row == 0, 0.0, pltpu.roll(d, 1, 0)) + jnp.where(
                row == CX - 1, 0.0, pltpu.roll(d, CX - 1, 0)
            )
            total = along_z[h] + along_x - 6.0 * d
            density = field[0, h, :, y, :]
            curvature = 34.0 + density * (192.0 * density - 192.0)
            work[0, h, :, y, :] = work[0, h, :, y, :] + (
                d * curvature
                - 2.0 * total
                - DT * got(h, (SLOTS + 1) * CX)
                - exists * value[h, 1 : CX + 1, PAD + y, :]
            )
            work[0, h, :, inner, :] = work[0, h, :, inner, :] - d
            twelve.append(12.0 * d)
        for s in range(1, NF):
            for h in BOTH:
                eta = field[s, h, :, y, :]
                change = DT * got(h, (s - 1) * CX) + twelve[h] * (eta * eta - eta)
                work[s, h, :, y, :] = work[s, h, :, y, :] + change
                if first_step:
                    sums[s - 1, h, y : y + 1, :] += jnp.sum(change, axis=0, keepdims=True)
        near = slice(0, 8) if y == 0 else slice(CY - 8, CY)
        store(slice(1, NF), slice(1, CX - 1), near)
        store(0, slice(2, CX - 2), near)

    for x, inner, present in ((0, 1, place[2]), (CX - 1, CX - 2, place[3])):

        def got(h, start, size):
            a = got_fa[h, start : start + size, :]
            b = got_fb[h, start : start + size, :]
            return jnp.where(even_x, b, a) if x == 0 else jnp.where(even_x, a, b)

        exists = present.astype(F32) * DT
        delta = []
        for h in BOTH:
            d = DT * got(h, SLOTS * CY, CY)
            delta.append(d)
            edge[h, 8 : 8 + CY, :] = d
            if first_step:
                edge[h, 0:8, :] = jnp.zeros((8, LN), F32)
                edge[h, 8 + CY : 16 + CY, :] = jnp.zeros((8, LN), F32)
            else:
                ends = DT * got(h, FACE, 8)
                edge[h, 7:8, :] = ends[0:1, :]
                edge[h, 8 + CY : 9 + CY, :] = ends[1:2, :]
        along_z = z_sum(*delta)
        twelve = []
        for h in BOTH:
            total = along_z[h] + edge[h, 9 : 9 + CY, :] + edge[h, 7 : 7 + CY, :] - 6.0 * delta[h]
            density = field[0, h, x]
            curvature = 34.0 + density * (192.0 * density - 192.0)
            work[0, h, x] += (
                delta[h] * curvature
                - 2.0 * total
                - DT * got(h, (SLOTS + 1) * CY, CY)
                - exists * value[h, x + 1, PAD : PAD + CY, :]
            )
            work[0, h, inner] -= delta[h]
            twelve.append(12.0 * delta[h])
        for s in range(1, NF):
            for h in BOTH:
                eta = field[s, h, x]
                change = DT * got(h, (s - 1) * CY, CY) + twelve[h] * (eta * eta - eta)
                work[s, h, x] += change
                if first_step:
                    sums[s - 1, h] += change
        store(slice(0, NF), x, slice(0, CY))
        store(0, inner, slice(0, CY))

    if first_step:
        for h in BOTH:
            for k in range(SLOTS + 2):
                s = k + 1 if k < SLOTS else 0
                depth = 1 if k == SLOTS + 1 else 0
                low, high = (work[s, h, x] for x in (depth, CX - 1 - depth))
                face_a[h, k * CY : (k + 1) * CY, :] = jnp.where(even_x, high, low)
                face_b[h, k * CY : (k + 1) * CY, :] = jnp.where(even_x, low, high)
                low, high = (work[s, h, :, y, :] for y in (depth, CY - 1 - depth))
                side_a[h, k * CX : (k + 1) * CX, :] = jnp.where(even_y, high, low)
                side_b[h, k * CX : (k + 1) * CX, :] = jnp.where(even_y, low, high)
            start = SLOTS * CY
            ends = []
            for at in (start, start + CY - 1):
                a, b = got_fa[h, at : at + 1, :], got_fb[h, at : at + 1, :]
                at_low, at_high = jnp.where(even_x, b, a), jnp.where(even_x, a, b)
                ends.append(jnp.where(row == 0, at_low, at_high))
            side_a[h, SIDE : SIDE + 8, :] = jnp.where(even_y, ends[1], ends[0])
            side_b[h, SIDE : SIDE + 8, :] = jnp.where(even_y, ends[0], ends[1])
    wait_all(stores)


def fix(place, value, field, got_faces, got_sides, base, out, sums=None):
    first_step = sums is not None
    args = [place, value, field, *got_faces, *got_sides, base, out]
    in_specs = [SM] + [VM] * 7 + [HBM]
    out_shape, out_specs = [BLOCK, WHOLE], [VM, HBM]
    aliases = {7: 0, 8: 1}
    if first_step:
        args.append(sums)
        in_specs.append(VM)
        out_shape += [SUMS] + [face_message(EXTRA)] * 2 + [side_message(EXTRA)] * 2
        out_specs += [VM] * 5
        aliases[9] = 2
    return pl.pallas_call(
        functools.partial(fix_kernel, first_step),
        out_shape=out_shape,
        in_specs=in_specs,
        out_specs=out_specs,
        scratch_shapes=[pltpu.VMEM((HALF, ROWS, LN), F32), pltpu.SemaphoreType.DMA((16,))],
        input_output_aliases=aliases,
        compiler_params=pltpu.CompilerParams(vmem_limit_bytes=LIMIT),
        name="fix",
    )(*args)[1:]


def grain_kernel(groups, grains, sums, rows):
    rows[...] = jnp.zeros(rows.shape, F32)
    row = lax.broadcasted_iota(jnp.int32, (GRAIN_DEV, LN), 0)
    for t in range(CY // 8):
        for s in range(SLOTS):
            grain = grains[0, t, s]
            start = pl.multiple_of(grain // (GRAIN_DEV * groups) * GRAIN_DEV, GRAIN_DEV)
            chosen = row == grain % GRAIN_DEV
            for h in range(HALF):
                total = DT * jnp.sum(sums[s, h, t * 8 : t * 8 + 8, :], axis=0, keepdims=True)
                rows[pl.ds(start, GRAIN_DEV), lanes(h)] += jnp.where(chosen, total, 0.0)


def grain_rows(slot_grain, sums, peers, groups):
    return pl.pallas_call(
        functools.partial(grain_kernel, groups),
        out_shape=jax.ShapeDtypeStruct((peers * GRAIN_DEV, NZ), F32),
        in_specs=[SM, VM],
        out_specs=VM,
        compiler_params=pltpu.CompilerParams(vmem_limit_bytes=LIMIT),
        name="grain_rows",
    )(slot_grain, sums)


def swaps(axis, count, first, second):
    near = [(i, i ^ 1) for i in range(count)]
    far = [(i, ((i + 1) ^ 1) - 1) for i in range(1, count - 1)]
    return lax.ppermute(first, axis, near), lax.ppermute(second, axis, far)


def shards(n_gx, n_gy, cotangent, fields_one, fields_zero, slot_grain):
    gx, gy = lax.axis_index("gx"), lax.axis_index("gy")
    cotangent, fields_one, fields_zero = (
        pltpu.with_memory_space_constraint(array, pltpu.HBM)
        for array in (cotangent, fields_one, fields_zero)
    )
    place = jnp.stack(
        [gx % 2, gy % 2, gx > 0, gx < n_gx - 1, gy > 0, gy < n_gy - 1]
    ).astype(jnp.int32)

    face_a, face_b, side_a, side_b = pack(place, cotangent)
    first_faces = swaps("gx", n_gx, face_a, face_b)
    got_sides = swaps("gy", n_gy, side_a, side_b)
    out, value, field, base, sums = local_step(cotangent, fields_one)
    costate, sums, face_a, face_b, side_a, side_b = fix(
        place, value, field, first_faces, got_sides, base, out, sums
    )

    got_sides = swaps("gy", n_gy, side_a, side_b)
    rows = grain_rows(slot_grain, sums, n_gx, n_gy)
    side_a, side_b, face_a, face_b, corners = corner(
        place, first_faces, rows, got_sides, (face_a, face_b)
    )
    got_faces = swaps("gx", n_gx, face_a, face_b)
    got_rows = lax.all_to_all(
        rows.reshape(n_gx, GRAIN_DEV, NZ), "gx", split_axis=0, concat_axis=0, tiled=True
    )
    costate = pltpu.with_memory_space_constraint(costate, pltpu.HBM)
    out, value, field, base = local_step(costate, fields_zero, corners)
    (adjoint,) = fix(place, value, field, got_faces, (side_a, side_b), base, out)
    got_rows, adjoint = lax.optimization_barrier((got_rows, adjoint))
    grain_grad = jnp.sum(got_rows.reshape(n_gx, GRAIN_DEV, NZ), axis=0)
    return adjoint, grain_grad


def solution(mesh):
    placed = (
        P(None, "gx", "gy", None),
        P(None, "gx", "gy", None),
        P(None, "gx", "gy", None),
        P("gx", "gy", None),
    )
    return jax.shard_map(
        functools.partial(shards, mesh.shape["gx"], mesh.shape["gy"]),
        mesh=mesh,
        in_specs=placed,
        out_specs=(P(None, "gx", "gy", None), P(("gx", "gy"), None)),
        check_vma=False,
    )
```

```python
import functools

import jax
import jax.numpy as jnp
from jax import lax
from jax.experimental import pallas as pl
from jax.experimental.pallas import tpu as pltpu
from jax.sharding import PartitionSpec as P

DT = 0.05
SLOTS = 8
NF = SLOTS + 1
CX, CY, NZ = 8, 64, 256
LN = 128
HALF = NZ // LN
GRAIN_DEV = 8
PAD = 8
ROWS = CY + 2 * PAD
FACE = (SLOTS + 2) * CY
SIDE = (SLOTS + 2) * CX
EXTRA = 8
F32 = jnp.float32
BOTH = range(HALF)
LIMIT = 4 << 20
HBM = pl.BlockSpec(memory_space=pltpu.HBM)
VM = pl.BlockSpec(memory_space=pltpu.VMEM)
SM = pl.BlockSpec(memory_space=pltpu.SMEM)


def lanes(half):
    return slice(half * LN, (half + 1) * LN)


def z_sum(first, second):
    lane = lax.broadcasted_iota(jnp.int32, first.shape, first.ndim - 1)
    axis = first.ndim - 1
    low, high = lane == 0, lane == LN - 1
    from_low = pltpu.roll(first, 1, axis)
    from_high = pltpu.roll(second, LN - 1, axis)
    left = jnp.where(low, 0.0, from_low), jnp.where(low, from_low, pltpu.roll(second, 1, axis))
    right = jnp.where(high, from_high, pltpu.roll(first, LN - 1, axis)), jnp.where(high, 0.0, from_high)
    return left[0] + right[0], left[1] + right[1]


def even_place():
    return tuple(lax.rem(lax.axis_index(axis), 2) == 0 for axis in ("gx", "gy"))


def has_neighbours(axis, count):
    index = lax.axis_index(axis)
    return tuple(jnp.where(beside, 1.0, 0.0) for beside in (index > 0, index < count - 1))


def start_all(copies):
    for copy in copies:
        copy.start()
    return copies


def wait_all(copies):
    for copy in copies:
        copy.wait()


def around(ref, x, row):
    own = [ref[h, x + 1, row : row + 8, :] for h in BOTH]
    along_z = z_sum(*own)
    total = [
        (ref[h, x, row : row + 8, :] + ref[h, x + 2, row : row + 8, :])
        + (ref[h, x + 1, row - 1 : row + 7, :] + ref[h, x + 1, row + 1 : row + 9, :])
        + along_z[h]
        for h in BOTH
    ]
    return own, total


def clear_edges(ref):
    tile = jnp.zeros((8, LN), F32)
    plane = jnp.zeros((CY, LN), F32)
    for h in BOTH:
        ref[h, 0, PAD : PAD + CY, :] = plane
        ref[h, CX + 1, PAD : PAD + CY, :] = plane
        for x in range(1, CX + 1):
            ref[h, x, 0:PAD, :] = tile
            ref[h, x, PAD + CY : ROWS, :] = tile


def local_kernel(with_sums, cos, fld, *rest):
    if with_sums:
        out, density_value, field, result, sums, *rest = rest
    else:
        corners, out, density_value, field, result, *rest = rest
    phases, potential, sem_c, sem_e, sem_f, sem_o, sem_d = rest

    def copy_c(h):
        return pltpu.make_async_copy(
            cos.at[0, :, :, lanes(h)],
            density_value.at[h, 1 : CX + 1, PAD : PAD + CY, :],
            sem_c.at[h],
        )

    def copy_e(x, h):
        return pltpu.make_async_copy(
            cos.at[1:NF, x, :, lanes(h)], phases.at[:, h, x + 1, PAD : PAD + CY, :], sem_e.at[x, h]
        )

    def copy_f(x, h):
        return pltpu.make_async_copy(fld.at[:, x, :, lanes(h)], field.at[:, h, x], sem_f.at[x, h])

    inside = slice(8, CY - 8)

    def copy_o(x, h):
        return pltpu.make_async_copy(
            result.at[1:NF, h, x, inside, :], out.at[1:NF, x, inside, lanes(h)], sem_o.at[x, h]
        )

    def copy_d(x, h):
        return pltpu.make_async_copy(
            result.at[0, h, x, inside, :], out.at[0, x, inside, lanes(h)], sem_d.at[x, h]
        )

    for h in BOTH:
        copy_c(h).start()
    for x in range(CX):
        for h in BOTH:
            copy_e(x, h).start()
            copy_f(x, h).start()

    clear_edges(potential)
    clear_edges(density_value)
    for s in range(SLOTS):
        clear_edges(phases.at[s])
    if with_sums:
        sums[...] = jnp.zeros(sums.shape, F32)
    for h in BOTH:
        copy_c(h).wait()
        if not with_sums:
            for edge, y in ((0, PAD), (8, PAD + CY - 1)):
                for k, x in ((0, 1), (1, CX)):
                    density_value[h, x, y : y + 1, :] += corners[h, edge + k : edge + k + 1, :]

    def potential_plane(x, carry):
        for part in range(CY // 8):
            row = PAD + part * 8
            own, total = around(density_value, x, row)
            for h in BOTH:
                potential[h, x + 1, row : row + 8, :] = DT * total[h] - (6.0 * DT) * own[h]
        return carry

    lax.fori_loop(0, CX, potential_plane, 0)

    for h in BOTH:
        copy_e(0, h).wait()

    def step_plane(x, carry):
        @pl.when(x < CX - 1)
        def _():
            for h in BOTH:
                copy_e(x + 1, h).wait()

        for h in BOTH:
            copy_f(x, h).wait()
        for part in range(CY // 8):
            row = PAD + part * 8
            here = slice(part * 8, part * 8 + 8)
            square = [None] * HALF
            weighted = [None] * HALF
            curved = [None] * HALF
            for s in range(SLOTS):
                for h in BOTH:
                    eta = field[s + 1, h, x, here, :]
                    lam = phases[s, h, x + 1, row : row + 8, :]
                    eta_eta = eta * eta
                    lam_eta = lam * eta
                    cubic = lam_eta * eta
                    square[h] = eta_eta if square[h] is None else square[h] + eta_eta
                    weighted[h] = lam_eta if weighted[h] is None else weighted[h] + lam_eta
                    curved[h] = cubic if curved[h] is None else curved[h] + cubic
            mu, mu_total = around(potential, x, row)
            scale, slope, mu_twelve, linear = [], [], [], []
            for h in BOTH:
                density = field[0, h, x, here, :]
                lam_c = density_value[h, x + 1, row : row + 8, :]
                curvature = 34.0 + density * (192.0 * density - 192.0)
                result[0, h, x, here, :] = (
                    lam_c
                    + mu[h] * (curvature + 6.0)
                    - mu_total[h]
                    - (12.0 * DT) * (curved[h] - weighted[h])
                )
                scale.append((1.0 - 18.0 * DT) + (12.0 * DT) * (density - square[h]))
                slope.append((48.0 * DT) - (24.0 * DT) * density)
                mu_twelve.append(12.0 * mu[h])
                linear.append((24.0 * DT) * weighted[h] + mu_twelve[h])
            for s in range(SLOTS):
                lam, total = around(phases.at[s], x, row)
                for h in BOTH:
                    eta = field[s + 1, h, x, here, :]
                    new = (
                        lam[h] * (scale[h] + slope[h] * eta)
                        + eta * (mu_twelve[h] * eta - linear[h])
                        + DT * total[h]
                    )
                    result[s + 1, h, x, here, :] = new
                    if with_sums:
                        sums[s, h, here, :] += lam[h] + new

        @pl.when((x > 0) & (x < CX - 1))
        def _():
            for h in BOTH:
                copy_o(x, h).start()

        @pl.when((x > 1) & (x < CX - 2))
        def _():
            for h in BOTH:
                copy_d(x, h).start()

        return carry

    lax.fori_loop(0, CX, step_plane, 0)
    for h in BOTH:
        for x in range(1, CX - 1):
            copy_o(x, h).wait()
        for x in range(2, CX - 2):
            copy_d(x, h).wait()


PADDED = jax.ShapeDtypeStruct((HALF, CX + 2, ROWS, LN), F32)
BLOCK = jax.ShapeDtypeStruct((NF, HALF, CX, CY, LN), F32)
SUMS = jax.ShapeDtypeStruct((SLOTS, HALF, CY, LN), F32)
WHOLE = pltpu.HBM((NF, CX, CY, NZ), F32)


def local_step(cos, fld, corners=None):
    with_sums = corners is None
    extra = [SUMS] if with_sums else []
    more = [] if with_sums else [corners]
    return pl.pallas_call(
        functools.partial(local_kernel, with_sums),
        out_shape=[WHOLE, PADDED, BLOCK, BLOCK] + extra,
        in_specs=[HBM, HBM] + [VM] * len(more),
        out_specs=[HBM, VM, VM, VM] + [VM] * len(extra),
        scratch_shapes=[
            pltpu.VMEM((SLOTS, HALF, CX + 2, ROWS, LN), F32),
            pltpu.VMEM((HALF, CX + 2, ROWS, LN), F32),
            pltpu.SemaphoreType.DMA((HALF,)),
            pltpu.SemaphoreType.DMA((CX, HALF)),
            pltpu.SemaphoreType.DMA((CX, HALF)),
            pltpu.SemaphoreType.DMA((CX, HALF)),
            pltpu.SemaphoreType.DMA((CX, HALF)),
        ],
        compiler_params=pltpu.CompilerParams(vmem_limit_bytes=12 << 20),
        cost_estimate=pl.CostEstimate(
            flops=250 * CX * CY * NZ, bytes_accessed=3 * 4 * NF * CX * CY * NZ, transcendentals=0
        ),
        name="local_step",
    )(cos, fld, *more)


def pack_kernel(cos, face_a, face_b, side_a, side_b, tiles, sem_p, sem_t):
    even_x, even_y = even_place()
    out_a = jnp.where(even_x, CX - 1, 0)
    in_a = jnp.where(even_x, CX - 2, 1)
    loads = start_all(
        [
            pltpu.make_async_copy(
                cos.at[:, :, edge * (CY - 8) : edge * (CY - 8) + 8, :], tiles.at[edge], sem_t.at[edge]
            )
            for edge in range(2)
        ]
    )
    copies = []
    for which, face, outer, inner in ((0, face_a, out_a, in_a), (1, face_b, CX - 1 - out_a, CX - 1 - in_a)):
        for h in BOTH:
            phases = face.at[h, 0 : SLOTS * CY, :].reshape(SLOTS, CY, LN)
            parts = (
                (cos.at[1:NF, outer, :, lanes(h)], phases),
                (cos.at[0, outer, :, lanes(h)], face.at[h, SLOTS * CY : SLOTS * CY + CY, :]),
                (cos.at[0, inner, :, lanes(h)], face.at[h, SLOTS * CY + CY : FACE, :]),
            )
            copies += [
                pltpu.make_async_copy(*part, sem_p.at[which, h, k]) for k, part in enumerate(parts)
            ]
    start_all(copies)
    wait_all(loads)
    for h in range(HALF):
        for k in range(SLOTS + 2):
            s = k + 1 if k < SLOTS else 0
            depth = 1 if k == SLOTS + 1 else 0
            low = tiles[0, s, :, depth, lanes(h)]
            high = tiles[1, s, :, 7 - depth, lanes(h)]
            side_a[h, k * CX : (k + 1) * CX, :] = jnp.where(even_y, high, low)
            side_b[h, k * CX : (k + 1) * CX, :] = jnp.where(even_y, low, high)
    wait_all(copies)


def face_message(extra):
    return jax.ShapeDtypeStruct((HALF, FACE + extra, LN), F32)


def side_message(extra):
    return jax.ShapeDtypeStruct((HALF, SIDE + extra, LN), F32)


def pack(cos):
    return pl.pallas_call(
        pack_kernel,
        out_shape=[face_message(0)] * 2 + [side_message(0)] * 2,
        in_specs=[HBM],
        out_specs=[VM] * 4,
        scratch_shapes=[
            pltpu.VMEM((2, NF, CX, 8, NZ), F32),
            pltpu.SemaphoreType.DMA((2, HALF, 3)),
            pltpu.SemaphoreType.DMA((2,)),
        ],
        compiler_params=pltpu.CompilerParams(vmem_limit_bytes=8 << 20),
        name="pack",
    )(cos)


def corner_kernel(sizes, first_a, first_b, order, got_a, got_b, face_a, face_b, *rest):
    del order, got_a, got_b, face_a, face_b
    side_a, side_b, out_a, out_b, corners = rest
    even_x, even_y = even_place()
    row = lax.broadcasted_iota(jnp.int32, (CX, LN), 0)
    face = slice(SLOTS * CX, SLOTS * CX + CX)
    start = SLOTS * CY
    for h in BOTH:
        ends_a = first_a[h, start : start + 1, :], first_a[h, start + CY - 1 : start + CY, :]
        ends_b = first_b[h, start : start + 1, :], first_b[h, start + CY - 1 : start + CY, :]
        fixed = []
        for ref, low_side in ((side_a, ~even_y), (side_b, even_y)):
            end_a = jnp.where(low_side, ends_a[0], ends_a[1])
            end_b = jnp.where(low_side, ends_b[0], ends_b[1])
            at_low = jnp.where(even_x, end_b, end_a)
            at_high = jnp.where(even_x, end_a, end_b)
            term = jnp.where(row == 0, at_low, jnp.where(row == CX - 1, at_high, 0.0))
            exists = jnp.where(low_side, *has_neighbours("gy", sizes[1]))
            value = ref[h, face, :] - (2.0 * DT * exists) * term
            ref[h, face, :] = value
            fixed.append(value)
        low = jnp.where(even_y, fixed[1], fixed[0])
        high = jnp.where(even_y, fixed[0], fixed[1])
        beyond_a, beyond_b = side_a[h, SIDE : SIDE + 8, :], side_b[h, SIDE : SIDE + 8, :]
        beyond_low = (-2.0 * DT) * jnp.where(even_y, beyond_b, beyond_a)
        beyond_high = (-2.0 * DT) * jnp.where(even_y, beyond_a, beyond_b)
        corners[h, 0:8, :] = beyond_low
        corners[h, 8:16, :] = beyond_high
        at_low = jnp.where(row == 0, low[0:1, :], high[0:1, :])
        at_high = jnp.where(row == 0, low[CX - 1 : CX, :], high[CX - 1 : CX, :])
        for ref, high_face in ((out_a, even_x), (out_b, ~even_x)):
            ref[h, FACE : FACE + 8, :] = jnp.where(high_face, at_high, at_low)
            ref[h, start : start + 1, :] += jnp.where(high_face, beyond_low[1:2, :], beyond_low[0:1, :])
            ref[h, start + CY - 1 : start + CY, :] += jnp.where(
                high_face, beyond_high[1:2, :], beyond_high[0:1, :]
            )


CORNERS = jax.ShapeDtypeStruct((HALF, 16, LN), F32)


def corner(sizes, first, order, got, faces):
    return pl.pallas_call(
        functools.partial(corner_kernel, sizes),
        out_shape=[side_message(EXTRA)] * 2 + [face_message(EXTRA)] * 2 + [CORNERS],
        in_specs=[VM, VM, HBM] + [VM] * 4,
        out_specs=[VM] * 5,
        input_output_aliases={3: 0, 4: 1, 5: 2, 6: 3},
        compiler_params=pltpu.CompilerParams(vmem_limit_bytes=LIMIT),
        name="corner",
    )(*first, order, *got, *faces)


def fix_kernel(sizes, first_step, value, field, got_fa, got_fb, got_sa, got_sb, *rest):
    if first_step:
        _, _, _, work, out, sums, face_a, face_b, side_a, side_b, edge, sem = rest
    else:
        _, _, work, out, edge, sem = rest
    even_x, even_y = even_place()
    near_x = has_neighbours("gx", sizes[0])
    near_y = has_neighbours("gy", sizes[1])
    stores = []

    def store(*where):
        s, x, y = where
        for h in BOTH:
            stores.append(
                pltpu.make_async_copy(work.at[s, h, x, y, :], out.at[s, x, y, lanes(h)], sem.at[len(stores)])
            )
            stores[-1].start()

    row = lax.broadcasted_iota(jnp.int32, (CX, LN), 0)
    for y, inner, present in ((0, 1, near_y[0]), (CY - 1, CY - 2, near_y[1])):

        def got(h, start):
            a = got_sa[h, start : start + CX, :]
            b = got_sb[h, start : start + CX, :]
            return jnp.where(even_y, b, a) if y == 0 else jnp.where(even_y, a, b)

        exists = present * DT
        delta = [DT * got(h, SLOTS * CX) for h in BOTH]
        along_z = z_sum(*delta)
        twelve = []
        for h in BOTH:
            d = delta[h]
            along_x = jnp.where(row == 0, 0.0, pltpu.roll(d, 1, 0)) + jnp.where(
                row == CX - 1, 0.0, pltpu.roll(d, CX - 1, 0)
            )
            total = along_z[h] + along_x - 6.0 * d
            density = field[0, h, :, y, :]
            curvature = 34.0 + density * (192.0 * density - 192.0)
            work[0, h, :, y, :] = work[0, h, :, y, :] + (
                d * curvature
                - 2.0 * total
                - DT * got(h, (SLOTS + 1) * CX)
                - exists * value[h, 1 : CX + 1, PAD + y, :]
            )
            work[0, h, :, inner, :] = work[0, h, :, inner, :] - d
            twelve.append(12.0 * d)
        for s in range(1, NF):
            for h in BOTH:
                eta = field[s, h, :, y, :]
                change = DT * got(h, (s - 1) * CX) + twelve[h] * (eta * eta - eta)
                work[s, h, :, y, :] = work[s, h, :, y, :] + change
                if first_step:
                    sums[s - 1, h, y : y + 1, :] += jnp.sum(change, axis=0, keepdims=True)
        near = slice(0, 8) if y == 0 else slice(CY - 8, CY)
        store(slice(1, NF), slice(1, CX - 1), near)
        store(0, slice(2, CX - 2), near)

    for x, inner, present in ((0, 1, near_x[0]), (CX - 1, CX - 2, near_x[1])):

        def got(h, start, size):
            a = got_fa[h, start : start + size, :]
            b = got_fb[h, start : start + size, :]
            return jnp.where(even_x, b, a) if x == 0 else jnp.where(even_x, a, b)

        exists = present * DT
        delta = []
        for h in BOTH:
            d = DT * got(h, SLOTS * CY, CY)
            delta.append(d)
            edge[h, 8 : 8 + CY, :] = d
            if first_step:
                edge[h, 0:8, :] = jnp.zeros((8, LN), F32)
                edge[h, 8 + CY : 16 + CY, :] = jnp.zeros((8, LN), F32)
            else:
                ends = DT * got(h, FACE, 8)
                edge[h, 7:8, :] = ends[0:1, :]
                edge[h, 8 + CY : 9 + CY, :] = ends[1:2, :]
        along_z = z_sum(*delta)
        twelve = []
        for h in BOTH:
            total = along_z[h] + edge[h, 9 : 9 + CY, :] + edge[h, 7 : 7 + CY, :] - 6.0 * delta[h]
            density = field[0, h, x]
            curvature = 34.0 + density * (192.0 * density - 192.0)
            work[0, h, x] += (
                delta[h] * curvature
                - 2.0 * total
                - DT * got(h, (SLOTS + 1) * CY, CY)
                - exists * value[h, x + 1, PAD : PAD + CY, :]
            )
            work[0, h, inner] -= delta[h]
            twelve.append(12.0 * delta[h])
        for s in range(1, NF):
            for h in BOTH:
                eta = field[s, h, x]
                change = DT * got(h, (s - 1) * CY, CY) + twelve[h] * (eta * eta - eta)
                work[s, h, x] += change
                if first_step:
                    sums[s - 1, h] += change
        store(slice(0, NF), x, slice(0, CY))
        store(0, inner, slice(0, CY))

    if first_step:
        for h in BOTH:
            for k in range(SLOTS + 2):
                s = k + 1 if k < SLOTS else 0
                depth = 1 if k == SLOTS + 1 else 0
                low, high = (work[s, h, x] for x in (depth, CX - 1 - depth))
                face_a[h, k * CY : (k + 1) * CY, :] = jnp.where(even_x, high, low)
                face_b[h, k * CY : (k + 1) * CY, :] = jnp.where(even_x, low, high)
                low, high = (work[s, h, :, y, :] for y in (depth, CY - 1 - depth))
                side_a[h, k * CX : (k + 1) * CX, :] = jnp.where(even_y, high, low)
                side_b[h, k * CX : (k + 1) * CX, :] = jnp.where(even_y, low, high)
            start = SLOTS * CY
            ends = []
            for at in (start, start + CY - 1):
                a, b = got_fa[h, at : at + 1, :], got_fb[h, at : at + 1, :]
                at_low, at_high = jnp.where(even_x, b, a), jnp.where(even_x, a, b)
                ends.append(jnp.where(row == 0, at_low, at_high))
            side_a[h, SIDE : SIDE + 8, :] = jnp.where(even_y, ends[1], ends[0])
            side_b[h, SIDE : SIDE + 8, :] = jnp.where(even_y, ends[0], ends[1])
    wait_all(stores)


def fix(sizes, value, field, got_faces, got_sides, base, out, sums=None):
    first_step = sums is not None
    args = [value, field, *got_faces, *got_sides, base, out]
    in_specs = [VM] * 7 + [HBM]
    out_shape, out_specs = [BLOCK, WHOLE], [VM, HBM]
    aliases = {6: 0, 7: 1}
    if first_step:
        args.append(sums)
        in_specs.append(VM)
        out_shape += [SUMS] + [face_message(EXTRA)] * 2 + [side_message(EXTRA)] * 2
        out_specs += [VM] * 5
        aliases[8] = 2
    return pl.pallas_call(
        functools.partial(fix_kernel, sizes, first_step),
        out_shape=out_shape,
        in_specs=in_specs,
        out_specs=out_specs,
        scratch_shapes=[pltpu.VMEM((HALF, ROWS, LN), F32), pltpu.SemaphoreType.DMA((16,))],
        input_output_aliases=aliases,
        compiler_params=pltpu.CompilerParams(vmem_limit_bytes=LIMIT),
        name="fix",
    )(*args)[1:]


def grain_kernel(groups, grains, sums, rows):
    rows[...] = jnp.zeros(rows.shape, F32)
    row = lax.broadcasted_iota(jnp.int32, (GRAIN_DEV, LN), 0)
    for t in range(CY // 8):
        for s in range(SLOTS):
            grain = grains[0, t, s]
            start = pl.multiple_of(grain // (GRAIN_DEV * groups) * GRAIN_DEV, GRAIN_DEV)
            chosen = row == grain % GRAIN_DEV
            for h in range(HALF):
                total = DT * jnp.sum(sums[s, h, t * 8 : t * 8 + 8, :], axis=0, keepdims=True)
                rows[pl.ds(start, GRAIN_DEV), lanes(h)] += jnp.where(chosen, total, 0.0)


def grain_rows(slot_grain, sums, peers, groups):
    return pl.pallas_call(
        functools.partial(grain_kernel, groups),
        out_shape=jax.ShapeDtypeStruct((peers * GRAIN_DEV, NZ), F32),
        in_specs=[SM, VM],
        out_specs=VM,
        compiler_params=pltpu.CompilerParams(vmem_limit_bytes=LIMIT),
        name="grain_rows",
    )(slot_grain, sums)


def swaps(axis, count, first, second):
    near = [(i, i ^ 1) for i in range(count)]
    far = [(i, ((i + 1) ^ 1) - 1) for i in range(1, count - 1)]
    return lax.ppermute(first, axis, near), lax.ppermute(second, axis, far)


def shards(n_gx, n_gy, cotangent, fields_one, fields_zero, slot_grain):
    sizes = n_gx, n_gy
    cotangent, fields_one, fields_zero = (
        pltpu.with_memory_space_constraint(array, pltpu.HBM)
        for array in (cotangent, fields_one, fields_zero)
    )
    face_a, face_b, side_a, side_b = pack(cotangent)
    first_faces = swaps("gx", n_gx, face_a, face_b)
    got_sides = swaps("gy", n_gy, side_a, side_b)
    out, value, field, base, sums = local_step(cotangent, fields_one)
    costate, sums, face_a, face_b, side_a, side_b = fix(
        sizes, value, field, first_faces, got_sides, base, out, sums
    )

    got_sides = swaps("gy", n_gy, side_a, side_b)
    rows = grain_rows(slot_grain, sums, n_gx, n_gy)
    side_a, side_b, face_a, face_b, corners = corner(
        sizes, first_faces, rows, got_sides, (face_a, face_b)
    )
    got_faces = swaps("gx", n_gx, face_a, face_b)
    got_rows = lax.all_to_all(
        rows.reshape(n_gx, GRAIN_DEV, NZ), "gx", split_axis=0, concat_axis=0, tiled=True
    )
    costate = pltpu.with_memory_space_constraint(costate, pltpu.HBM)
    out, value, field, base = local_step(costate, fields_zero, corners)
    (adjoint,) = fix(sizes, value, field, got_faces, (side_a, side_b), base, out)
    got_rows, adjoint = lax.optimization_barrier((got_rows, adjoint))
    grain_grad = jnp.sum(got_rows.reshape(n_gx, GRAIN_DEV, NZ), axis=0)
    return adjoint, grain_grad


def solution(mesh):
    placed = (
        P(None, "gx", "gy", None),
        P(None, "gx", "gy", None),
        P(None, "gx", "gy", None),
        P("gx", "gy", None),
    )
    return jax.shard_map(
        functools.partial(shards, mesh.shape["gx"], mesh.shape["gy"]),
        mesh=mesh,
        in_specs=placed,
        out_specs=(P(None, "gx", "gy", None), P(("gx", "gy"), None)),
        check_vma=False,
    )
```

```python
import functools

import jax
import jax.numpy as jnp
from jax import lax
from jax.experimental import pallas as pl
from jax.experimental.pallas import tpu as pltpu
from jax.sharding import PartitionSpec as P

DT = 0.05
SLOTS = 8
NF = SLOTS + 1
CX, CY, NZ = 8, 64, 256
LN = 128
HALF = NZ // LN
GRAIN_DEV = 8
PAD = 8
ROWS = CY + 2 * PAD
FACE = (SLOTS + 2) * CY
SIDE = (SLOTS + 2) * CX
EXTRA = 8
F32 = jnp.float32
BOTH = range(HALF)
LIMIT = 4 << 20
HBM = pl.BlockSpec(memory_space=pltpu.HBM)
VM = pl.BlockSpec(memory_space=pltpu.VMEM)
SM = pl.BlockSpec(memory_space=pltpu.SMEM)


def lanes(half):
    return slice(half * LN, (half + 1) * LN)


def z_sum(first, second):
    lane = lax.broadcasted_iota(jnp.int32, first.shape, first.ndim - 1)
    axis = first.ndim - 1
    low, high = lane == 0, lane == LN - 1
    from_low = pltpu.roll(first, 1, axis)
    from_high = pltpu.roll(second, LN - 1, axis)
    left = jnp.where(low, 0.0, from_low), jnp.where(low, from_low, pltpu.roll(second, 1, axis))
    right = jnp.where(high, from_high, pltpu.roll(first, LN - 1, axis)), jnp.where(high, 0.0, from_high)
    return left[0] + right[0], left[1] + right[1]


def even_place():
    return tuple(lax.rem(lax.axis_index(axis), 2) == 0 for axis in ("gx", "gy"))


def has_neighbours(axis, count):
    index = lax.axis_index(axis)
    return tuple(jnp.where(beside, 1.0, 0.0) for beside in (index > 0, index < count - 1))


def start_all(copies):
    for copy in copies:
        copy.start()
    return copies


def wait_all(copies):
    for copy in copies:
        copy.wait()


def around(ref, x, row):
    own = [ref[h, x + 1, row : row + 8, :] for h in BOTH]
    along_z = z_sum(*own)
    total = [
        (ref[h, x, row : row + 8, :] + ref[h, x + 2, row : row + 8, :])
        + (ref[h, x + 1, row - 1 : row + 7, :] + ref[h, x + 1, row + 1 : row + 9, :])
        + along_z[h]
        for h in BOTH
    ]
    return own, total


def clear_edges(ref):
    tile = jnp.zeros((8, LN), F32)
    plane = jnp.zeros((CY, LN), F32)
    for h in BOTH:
        ref[h, 0, PAD : PAD + CY, :] = plane
        ref[h, CX + 1, PAD : PAD + CY, :] = plane
        for x in range(1, CX + 1):
            ref[h, x, 0:PAD, :] = tile
            ref[h, x, PAD + CY : ROWS, :] = tile


def local_kernel(with_sums, cos, fld, *rest):
    if with_sums:
        out, density_value, field, result, sums, *rest = rest
    else:
        corners, out, density_value, field, result, *rest = rest
    phases, potential, sem_c, sem_e, sem_f, sem_o, sem_d = rest

    def copy_c(h):
        return pltpu.make_async_copy(
            cos.at[0, :, :, lanes(h)],
            density_value.at[h, 1 : CX + 1, PAD : PAD + CY, :],
            sem_c.at[h],
        )

    def copy_e(x, h):
        return pltpu.make_async_copy(
            cos.at[1:NF, x, :, lanes(h)], phases.at[:, h, x + 1, PAD : PAD + CY, :], sem_e.at[x, h]
        )

    def copy_f(x, h):
        return pltpu.make_async_copy(fld.at[:, x, :, lanes(h)], field.at[:, h, x], sem_f.at[x, h])

    inside = slice(8, CY - 8)

    def copy_o(x, h):
        return pltpu.make_async_copy(
            result.at[1:NF, h, x, inside, :], out.at[1:NF, x, inside, lanes(h)], sem_o.at[x, h]
        )

    def copy_d(x, h):
        return pltpu.make_async_copy(
            result.at[0, h, x, inside, :], out.at[0, x, inside, lanes(h)], sem_d.at[x, h]
        )

    for h in BOTH:
        copy_c(h).start()
    for x in range(CX):
        for h in BOTH:
            copy_e(x, h).start()
            copy_f(x, h).start()

    clear_edges(potential)
    clear_edges(density_value)
    for s in range(SLOTS):
        clear_edges(phases.at[s])
    if with_sums:
        sums[...] = jnp.zeros(sums.shape, F32)
    for h in BOTH:
        copy_c(h).wait()
        if not with_sums:
            for edge, y in ((0, PAD), (8, PAD + CY - 1)):
                for k, x in ((0, 1), (1, CX)):
                    density_value[h, x, y : y + 1, :] += corners[h, edge + k : edge + k + 1, :]

    def potential_plane(x, carry):
        for part in range(CY // 8):
            row = PAD + part * 8
            own, total = around(density_value, x, row)
            for h in BOTH:
                potential[h, x + 1, row : row + 8, :] = DT * total[h] - (6.0 * DT) * own[h]
        return carry

    lax.fori_loop(0, CX, potential_plane, 0)

    for h in BOTH:
        copy_e(0, h).wait()

    def step_plane(x, carry):
        @pl.when(x < CX - 1)
        def _():
            for h in BOTH:
                copy_e(x + 1, h).wait()

        for h in BOTH:
            copy_f(x, h).wait()
        for part in range(CY // 8):
            row = PAD + part * 8
            here = slice(part * 8, part * 8 + 8)
            square = [None] * HALF
            weighted = [None] * HALF
            curved = [None] * HALF
            for s in range(SLOTS):
                for h in BOTH:
                    eta = field[s + 1, h, x, here, :]
                    lam = phases[s, h, x + 1, row : row + 8, :]
                    eta_eta = eta * eta
                    lam_eta = lam * eta
                    cubic = lam_eta * eta
                    square[h] = eta_eta if square[h] is None else square[h] + eta_eta
                    weighted[h] = lam_eta if weighted[h] is None else weighted[h] + lam_eta
                    curved[h] = cubic if curved[h] is None else curved[h] + cubic
            mu, mu_total = around(potential, x, row)
            scale, slope, mu_twelve, linear = [], [], [], []
            for h in BOTH:
                density = field[0, h, x, here, :]
                lam_c = density_value[h, x + 1, row : row + 8, :]
                curvature = 34.0 + density * (192.0 * density - 192.0)
                result[0, h, x, here, :] = (
                    lam_c
                    + mu[h] * (curvature + 6.0)
                    - mu_total[h]
                    - (12.0 * DT) * (curved[h] - weighted[h])
                )
                scale.append((1.0 - 18.0 * DT) + (12.0 * DT) * (density - square[h]))
                slope.append((48.0 * DT) - (24.0 * DT) * density)
                mu_twelve.append(12.0 * mu[h])
                linear.append((24.0 * DT) * weighted[h] + mu_twelve[h])
            for s in range(SLOTS):
                lam, total = around(phases.at[s], x, row)
                for h in BOTH:
                    eta = field[s + 1, h, x, here, :]
                    new = (
                        lam[h] * (scale[h] + slope[h] * eta)
                        + eta * (mu_twelve[h] * eta - linear[h])
                        + DT * total[h]
                    )
                    result[s + 1, h, x, here, :] = new
                    if with_sums:
                        sums[s, h, here, :] += lam[h] + new

        @pl.when((x > 0) & (x < CX - 1))
        def _():
            for h in BOTH:
                copy_o(x, h).start()

        @pl.when((x > 1) & (x < CX - 2))
        def _():
            for h in BOTH:
                copy_d(x, h).start()

        return carry

    lax.fori_loop(0, CX, step_plane, 0)
    for h in BOTH:
        for x in range(1, CX - 1):
            copy_o(x, h).wait()
        for x in range(2, CX - 2):
            copy_d(x, h).wait()


PADDED = jax.ShapeDtypeStruct((HALF, CX + 2, ROWS, LN), F32)
BLOCK = jax.ShapeDtypeStruct((NF, HALF, CX, CY, LN), F32)
SUMS = jax.ShapeDtypeStruct((SLOTS, HALF, CY, LN), F32)
WHOLE = pltpu.HBM((NF, CX, CY, NZ), F32)


def local_step(cos, fld, corners=None):
    with_sums = corners is None
    extra = [SUMS] if with_sums else []
    more = [] if with_sums else [corners]
    return pl.pallas_call(
        functools.partial(local_kernel, with_sums),
        out_shape=[WHOLE, PADDED, BLOCK, BLOCK] + extra,
        in_specs=[HBM, HBM] + [VM] * len(more),
        out_specs=[HBM, VM, VM, VM] + [VM] * len(extra),
        scratch_shapes=[
            pltpu.VMEM((SLOTS, HALF, CX + 2, ROWS, LN), F32),
            pltpu.VMEM((HALF, CX + 2, ROWS, LN), F32),
            pltpu.SemaphoreType.DMA((HALF,)),
            pltpu.SemaphoreType.DMA((CX, HALF)),
            pltpu.SemaphoreType.DMA((CX, HALF)),
            pltpu.SemaphoreType.DMA((CX, HALF)),
            pltpu.SemaphoreType.DMA((CX, HALF)),
        ],
        compiler_params=pltpu.CompilerParams(vmem_limit_bytes=12 << 20),
        cost_estimate=pl.CostEstimate(
            flops=250 * CX * CY * NZ, bytes_accessed=3 * 4 * NF * CX * CY * NZ, transcendentals=0
        ),
        name="local_step",
    )(cos, fld, *more)


def pack_kernel(cos, face_a, face_b, side_a, side_b, tiles, sem_p, sem_t):
    even_x, even_y = even_place()
    out_a = jnp.where(even_x, CX - 1, 0)
    in_a = jnp.where(even_x, CX - 2, 1)
    loads = start_all(
        [
            pltpu.make_async_copy(
                cos.at[:, :, edge * (CY - 8) : edge * (CY - 8) + 8, :], tiles.at[edge], sem_t.at[edge]
            )
            for edge in range(2)
        ]
    )
    copies = []
    for which, face, outer, inner in ((0, face_a, out_a, in_a), (1, face_b, CX - 1 - out_a, CX - 1 - in_a)):
        for h in BOTH:
            phases = face.at[h, 0 : SLOTS * CY, :].reshape(SLOTS, CY, LN)
            parts = (
                (cos.at[1:NF, outer, :, lanes(h)], phases),
                (cos.at[0, outer, :, lanes(h)], face.at[h, SLOTS * CY : SLOTS * CY + CY, :]),
                (cos.at[0, inner, :, lanes(h)], face.at[h, SLOTS * CY + CY : FACE, :]),
            )
            copies += [
                pltpu.make_async_copy(*part, sem_p.at[which, h, k]) for k, part in enumerate(parts)
            ]
    start_all(copies)
    wait_all(loads)
    for h in range(HALF):
        for k in range(SLOTS + 2):
            s = k + 1 if k < SLOTS else 0
            depth = 1 if k == SLOTS + 1 else 0
            low = tiles[0, s, :, depth, lanes(h)]
            high = tiles[1, s, :, 7 - depth, lanes(h)]
            side_a[h, k * CX : (k + 1) * CX, :] = jnp.where(even_y, high, low)
            side_b[h, k * CX : (k + 1) * CX, :] = jnp.where(even_y, low, high)
    wait_all(copies)


def face_message(extra):
    return jax.ShapeDtypeStruct((HALF, FACE + extra, LN), F32)


def side_message(extra):
    return jax.ShapeDtypeStruct((HALF, SIDE + extra, LN), F32)


def pack(cos):
    return pl.pallas_call(
        pack_kernel,
        out_shape=[face_message(0)] * 2 + [side_message(0)] * 2,
        in_specs=[HBM],
        out_specs=[VM] * 4,
        scratch_shapes=[
            pltpu.VMEM((2, NF, CX, 8, NZ), F32),
            pltpu.SemaphoreType.DMA((2, HALF, 3)),
            pltpu.SemaphoreType.DMA((2,)),
        ],
        compiler_params=pltpu.CompilerParams(vmem_limit_bytes=8 << 20),
        name="pack",
    )(cos)


def corner_kernel(sizes, first_a, first_b, order, got_a, got_b, face_a, face_b, *rest):
    del order, got_a, got_b, face_a, face_b
    side_a, side_b, out_a, out_b, corners = rest
    even_x, even_y = even_place()
    row = lax.broadcasted_iota(jnp.int32, (CX, LN), 0)
    face = slice(SLOTS * CX, SLOTS * CX + CX)
    start = SLOTS * CY
    for h in BOTH:
        ends_a = first_a[h, start : start + 1, :], first_a[h, start + CY - 1 : start + CY, :]
        ends_b = first_b[h, start : start + 1, :], first_b[h, start + CY - 1 : start + CY, :]
        fixed = []
        for ref, low_side in ((side_a, ~even_y), (side_b, even_y)):
            end_a = jnp.where(low_side, ends_a[0], ends_a[1])
            end_b = jnp.where(low_side, ends_b[0], ends_b[1])
            at_low = jnp.where(even_x, end_b, end_a)
            at_high = jnp.where(even_x, end_a, end_b)
            term = jnp.where(row == 0, at_low, jnp.where(row == CX - 1, at_high, 0.0))
            exists = jnp.where(low_side, *has_neighbours("gy", sizes[1]))
            value = ref[h, face, :] - (2.0 * DT * exists) * term
            ref[h, face, :] = value
            fixed.append(value)
        low = jnp.where(even_y, fixed[1], fixed[0])
        high = jnp.where(even_y, fixed[0], fixed[1])
        beyond_a, beyond_b = side_a[h, SIDE : SIDE + 8, :], side_b[h, SIDE : SIDE + 8, :]
        beyond_low = (-2.0 * DT) * jnp.where(even_y, beyond_b, beyond_a)
        beyond_high = (-2.0 * DT) * jnp.where(even_y, beyond_a, beyond_b)
        corners[h, 0:8, :] = beyond_low
        corners[h, 8:16, :] = beyond_high
        at_low = jnp.where(row == 0, low[0:1, :], high[0:1, :])
        at_high = jnp.where(row == 0, low[CX - 1 : CX, :], high[CX - 1 : CX, :])
        for ref, high_face in ((out_a, even_x), (out_b, ~even_x)):
            ref[h, FACE : FACE + 8, :] = jnp.where(high_face, at_high, at_low)
            ref[h, start : start + 1, :] += jnp.where(high_face, beyond_low[1:2, :], beyond_low[0:1, :])
            ref[h, start + CY - 1 : start + CY, :] += jnp.where(
                high_face, beyond_high[1:2, :], beyond_high[0:1, :]
            )


CORNERS = jax.ShapeDtypeStruct((HALF, 16, LN), F32)


def corner(sizes, first, order, got, faces):
    return pl.pallas_call(
        functools.partial(corner_kernel, sizes),
        out_shape=[side_message(EXTRA)] * 2 + [face_message(EXTRA)] * 2 + [CORNERS],
        in_specs=[VM, VM, HBM] + [VM] * 4,
        out_specs=[VM] * 5,
        input_output_aliases={3: 0, 4: 1, 5: 2, 6: 3},
        compiler_params=pltpu.CompilerParams(vmem_limit_bytes=LIMIT),
        name="corner",
    )(*first, order, *got, *faces)


def grain_rows(groups, grains, sums, rows):
    rows[...] = jnp.zeros(rows.shape, F32)
    row = lax.broadcasted_iota(jnp.int32, (GRAIN_DEV, LN), 0)
    for t in range(CY // 8):
        for s in range(SLOTS):
            grain = grains[0, t, s]
            start = pl.multiple_of(grain // (GRAIN_DEV * groups) * GRAIN_DEV, GRAIN_DEV)
            chosen = row == grain % GRAIN_DEV
            for h in range(HALF):
                total = DT * jnp.sum(sums[s, h, t * 8 : t * 8 + 8, :], axis=0, keepdims=True)
                rows[pl.ds(start, GRAIN_DEV), lanes(h)] += jnp.where(chosen, total, 0.0)


def fix_kernel(sizes, stage, *refs):
    sums = None
    if stage == "early":
        value, field, got_fa, got_fb, got_sa, got_sb, _, _, work, sums, side_a, side_b, edge = refs
        spans = (slice(0, 8), slice(CY - 8, CY))
    elif stage == "late":
        grains, value, field, got_fa, got_fb, _, _, _, work, out, sums, face_a, face_b, rows, edge, sem = refs
        spans = (slice(8, CY - 8),)
    else:
        value, field, got_fa, got_fb, got_sa, got_sb, _, _, work, out, edge, sem = refs
        spans = (slice(0, CY),)
    even_x, even_y = even_place()
    near_x = has_neighbours("gx", sizes[0])
    near_y = has_neighbours("gy", sizes[1])
    stores = []

    def store(*where):
        s, x, y = where
        for h in BOTH if stage != "early" else ():
            stores.append(
                pltpu.make_async_copy(work.at[s, h, x, y, :], out.at[s, x, y, lanes(h)], sem.at[len(stores)])
            )
            stores[-1].start()

    row = lax.broadcasted_iota(jnp.int32, (CX, LN), 0)
    for y, inner, present in ((0, 1, near_y[0]), (CY - 1, CY - 2, near_y[1])):
        near = slice(0, 8) if y == 0 else slice(CY - 8, CY)
        if stage == "late":
            store(slice(1, NF), slice(1, CX - 1), near)
            store(0, slice(2, CX - 2), near)
            continue

        def got(h, start):
            a = got_sa[h, start : start + CX, :]
            b = got_sb[h, start : start + CX, :]
            return jnp.where(even_y, b, a) if y == 0 else jnp.where(even_y, a, b)

        exists = present * DT
        delta = [DT * got(h, SLOTS * CX) for h in BOTH]
        along_z = z_sum(*delta)
        twelve = []
        for h in BOTH:
            d = delta[h]
            along_x = jnp.where(row == 0, 0.0, pltpu.roll(d, 1, 0)) + jnp.where(
                row == CX - 1, 0.0, pltpu.roll(d, CX - 1, 0)
            )
            total = along_z[h] + along_x - 6.0 * d
            density = field[0, h, :, y, :]
            curvature = 34.0 + density * (192.0 * density - 192.0)
            work[0, h, :, y, :] = work[0, h, :, y, :] + (
                d * curvature
                - 2.0 * total
                - DT * got(h, (SLOTS + 1) * CX)
                - exists * value[h, 1 : CX + 1, PAD + y, :]
            )
            work[0, h, :, inner, :] = work[0, h, :, inner, :] - d
            twelve.append(12.0 * d)
        for s in range(1, NF):
            for h in BOTH:
                eta = field[s, h, :, y, :]
                change = DT * got(h, (s - 1) * CX) + twelve[h] * (eta * eta - eta)
                work[s, h, :, y, :] = work[s, h, :, y, :] + change
                if sums is not None:
                    sums[s - 1, h, y : y + 1, :] += jnp.sum(change, axis=0, keepdims=True)
        store(slice(1, NF), slice(1, CX - 1), near)
        store(0, slice(2, CX - 2), near)

    for x, inner, present in ((0, 1, near_x[0]), (CX - 1, CX - 2, near_x[1])):

        def got(h, start, size):
            a = got_fa[h, start : start + size, :]
            b = got_fb[h, start : start + size, :]
            return jnp.where(even_x, b, a) if x == 0 else jnp.where(even_x, a, b)

        exists = present * DT
        delta = []
        for h in BOTH:
            d = DT * got(h, SLOTS * CY, CY)
            delta.append(d)
            edge[h, 8 : 8 + CY, :] = d
            if sums is not None:
                edge[h, 0:8, :] = jnp.zeros((8, LN), F32)
                edge[h, 8 + CY : 16 + CY, :] = jnp.zeros((8, LN), F32)
            else:
                ends = DT * got(h, FACE, 8)
                edge[h, 7:8, :] = ends[0:1, :]
                edge[h, 8 + CY : 9 + CY, :] = ends[1:2, :]
        for span in spans:
            size = span.stop - span.start
            part = [d[span] for d in delta]
            along_z = z_sum(*part)
            twelve = []
            for h in BOTH:
                above = edge[h, 9 + span.start : 9 + span.stop, :]
                below = edge[h, 7 + span.start : 7 + span.stop, :]
                total = along_z[h] + above + below - 6.0 * part[h]
                density = field[0, h, x, span, :]
                curvature = 34.0 + density * (192.0 * density - 192.0)
                work[0, h, x, span, :] += (
                    part[h] * curvature
                    - 2.0 * total
                    - DT * got(h, (SLOTS + 1) * CY + span.start, size)
                    - exists * value[h, x + 1, PAD + span.start : PAD + span.stop, :]
                )
                work[0, h, inner, span, :] -= part[h]
                twelve.append(12.0 * part[h])
            for s in range(1, NF):
                for h in BOTH:
                    eta = field[s, h, x, span, :]
                    change = DT * got(h, (s - 1) * CY + span.start, size) + twelve[h] * (eta * eta - eta)
                    work[s, h, x, span, :] += change
                    if sums is not None:
                        sums[s - 1, h, span, :] += change
        store(slice(0, NF), x, slice(0, CY))
        store(0, inner, slice(0, CY))

    for h in BOTH:
        for k in range(SLOTS + 2):
            s = k + 1 if k < SLOTS else 0
            depth = 1 if k == SLOTS + 1 else 0
            if stage == "late":
                low, high = (work[s, h, x] for x in (depth, CX - 1 - depth))
                face_a[h, k * CY : (k + 1) * CY, :] = jnp.where(even_x, high, low)
                face_b[h, k * CY : (k + 1) * CY, :] = jnp.where(even_x, low, high)
            if stage == "early":
                low, high = (work[s, h, :, y, :] for y in (depth, CY - 1 - depth))
                side_a[h, k * CX : (k + 1) * CX, :] = jnp.where(even_y, high, low)
                side_b[h, k * CX : (k + 1) * CX, :] = jnp.where(even_y, low, high)
        if stage == "early":
            start = SLOTS * CY
            ends = []
            for at in (start, start + CY - 1):
                a, b = got_fa[h, at : at + 1, :], got_fb[h, at : at + 1, :]
                at_low, at_high = jnp.where(even_x, b, a), jnp.where(even_x, a, b)
                ends.append(jnp.where(row == 0, at_low, at_high))
            side_a[h, SIDE : SIDE + 8, :] = jnp.where(even_y, ends[1], ends[0])
            side_b[h, SIDE : SIDE + 8, :] = jnp.where(even_y, ends[0], ends[1])
    if stage == "late":
        grain_rows(sizes[1], grains, sums, rows)
    wait_all(stores)


EDGE = pltpu.VMEM((HALF, ROWS, LN), F32)
STORES = pltpu.SemaphoreType.DMA((16,))


def fix_early(sizes, value, field, got_faces, got_sides, base, sums):
    return pl.pallas_call(
        functools.partial(fix_kernel, sizes, "early"),
        out_shape=[BLOCK, SUMS] + [side_message(EXTRA)] * 2,
        in_specs=[VM] * 8,
        out_specs=[VM] * 4,
        scratch_shapes=[EDGE],
        input_output_aliases={6: 0, 7: 1},
        compiler_params=pltpu.CompilerParams(vmem_limit_bytes=LIMIT),
        name="fix_early",
    )(value, field, *got_faces, *got_sides, base, sums)


def fix_late(sizes, slot_grain, value, field, got_faces, base, out, sums):
    rows = jax.ShapeDtypeStruct((sizes[0] * GRAIN_DEV, NZ), F32)
    return pl.pallas_call(
        functools.partial(fix_kernel, sizes, "late"),
        out_shape=[BLOCK, WHOLE, SUMS] + [face_message(EXTRA)] * 2 + [rows],
        in_specs=[SM] + [VM] * 5 + [HBM, VM],
        out_specs=[VM, HBM] + [VM] * 4,
        scratch_shapes=[EDGE, STORES],
        input_output_aliases={5: 0, 6: 1, 7: 2},
        compiler_params=pltpu.CompilerParams(vmem_limit_bytes=LIMIT),
        name="fix_late",
    )(slot_grain, value, field, *got_faces, base, out, sums)


def fix_whole(sizes, value, field, got_faces, got_sides, base, out):
    return pl.pallas_call(
        functools.partial(fix_kernel, sizes, "whole"),
        out_shape=[BLOCK, WHOLE],
        in_specs=[VM] * 7 + [HBM],
        out_specs=[VM, HBM],
        scratch_shapes=[EDGE, STORES],
        input_output_aliases={6: 0, 7: 1},
        compiler_params=pltpu.CompilerParams(vmem_limit_bytes=LIMIT),
        name="fix_whole",
    )(value, field, *got_faces, *got_sides, base, out)[1]


def swaps(axis, count, first, second):
    near = [(i, i ^ 1) for i in range(count)]
    far = [(i, ((i + 1) ^ 1) - 1) for i in range(1, count - 1)]
    return lax.ppermute(first, axis, near), lax.ppermute(second, axis, far)


def shards(n_gx, n_gy, cotangent, fields_one, fields_zero, slot_grain):
    sizes = n_gx, n_gy
    cotangent, fields_one, fields_zero = (
        pltpu.with_memory_space_constraint(array, pltpu.HBM)
        for array in (cotangent, fields_one, fields_zero)
    )
    face_a, face_b, side_a, side_b = pack(cotangent)
    first_faces = swaps("gx", n_gx, face_a, face_b)
    got_sides = swaps("gy", n_gy, side_a, side_b)
    out, value, field, base, sums = local_step(cotangent, fields_one)
    base, sums, side_a, side_b = fix_early(sizes, value, field, first_faces, got_sides, base, sums)

    got_sides = swaps("gy", n_gy, side_a, side_b)
    _, costate, _, face_a, face_b, rows = fix_late(
        sizes, slot_grain, value, field, first_faces, base, out, sums
    )
    side_a, side_b, face_a, face_b, corners = corner(
        sizes, first_faces, rows, got_sides, (face_a, face_b)
    )
    got_faces = swaps("gx", n_gx, face_a, face_b)
    got_rows = lax.all_to_all(
        rows.reshape(n_gx, GRAIN_DEV, NZ), "gx", split_axis=0, concat_axis=0, tiled=True
    )
    costate = pltpu.with_memory_space_constraint(costate, pltpu.HBM)
    out, value, field, base = local_step(costate, fields_zero, corners)
    adjoint = fix_whole(sizes, value, field, got_faces, (side_a, side_b), base, out)
    got_rows, adjoint = lax.optimization_barrier((got_rows, adjoint))
    grain_grad = jnp.sum(got_rows.reshape(n_gx, GRAIN_DEV, NZ), axis=0)
    return adjoint, grain_grad


def solution(mesh):
    placed = (
        P(None, "gx", "gy", None),
        P(None, "gx", "gy", None),
        P(None, "gx", "gy", None),
        P("gx", "gy", None),
    )
    return jax.shard_map(
        functools.partial(shards, mesh.shape["gx"], mesh.shape["gy"]),
        mesh=mesh,
        in_specs=placed,
        out_specs=(P(None, "gx", "gy", None), P(("gx", "gy"), None)),
        check_vma=False,
    )
```

```python
import functools

import jax
import jax.numpy as jnp
from jax import lax
from jax.experimental import pallas as pl
from jax.experimental.pallas import tpu as pltpu
from jax.sharding import PartitionSpec as P

DT = 0.05
SLOTS = 8
NF = SLOTS + 1
CX, CY, NZ = 8, 64, 256
LN = 128
HALF = NZ // LN
GRAIN_DEV = 8
PAD = 8
ROWS = CY + 2 * PAD
FACE = (SLOTS + 2) * CY
SIDE = (SLOTS + 2) * CX
EXTRA = 8
F32 = jnp.float32
BOTH = range(HALF)
LIMIT = 4 << 20
HBM = pl.BlockSpec(memory_space=pltpu.HBM)
VM = pl.BlockSpec(memory_space=pltpu.VMEM)
SM = pl.BlockSpec(memory_space=pltpu.SMEM)


def lanes(half):
    return slice(half * LN, (half + 1) * LN)


def z_sum(first, second):
    lane = lax.broadcasted_iota(jnp.int32, first.shape, first.ndim - 1)
    axis = first.ndim - 1
    low, high = lane == 0, lane == LN - 1
    from_low = pltpu.roll(first, 1, axis)
    from_high = pltpu.roll(second, LN - 1, axis)
    left = jnp.where(low, 0.0, from_low), jnp.where(low, from_low, pltpu.roll(second, 1, axis))
    right = jnp.where(high, from_high, pltpu.roll(first, LN - 1, axis)), jnp.where(high, 0.0, from_high)
    return left[0] + right[0], left[1] + right[1]


def even_place():
    return tuple(lax.rem(lax.axis_index(axis), 2) == 0 for axis in ("gx", "gy"))


def has_neighbours(axis, count):
    index = lax.axis_index(axis)
    return tuple(jnp.where(beside, 1.0, 0.0) for beside in (index > 0, index < count - 1))


def start_all(copies):
    for copy in copies:
        copy.start()
    return copies


def wait_all(copies):
    for copy in copies:
        copy.wait()


def around(ref, x, row):
    own = [ref[h, x + 1, row : row + 8, :] for h in BOTH]
    along_z = z_sum(*own)
    total = [
        (ref[h, x, row : row + 8, :] + ref[h, x + 2, row : row + 8, :])
        + (ref[h, x + 1, row - 1 : row + 7, :] + ref[h, x + 1, row + 1 : row + 9, :])
        + along_z[h]
        for h in BOTH
    ]
    return own, total


def clear_edges(ref):
    tile = jnp.zeros((8, LN), F32)
    plane = jnp.zeros((CY, LN), F32)
    for h in BOTH:
        ref[h, 0, PAD : PAD + CY, :] = plane
        ref[h, CX + 1, PAD : PAD + CY, :] = plane
        for x in range(1, CX + 1):
            ref[h, x, 0:PAD, :] = tile
            ref[h, x, PAD + CY : ROWS, :] = tile


def local_kernel(with_sums, cos, fld, *rest):
    if with_sums:
        out, density_value, field, result, sums, *rest = rest
    else:
        corners, out, density_value, field, result, *rest = rest
    phases, potential, sem_c, sem_e, sem_f, sem_o, sem_d = rest

    def copy_c(h):
        return pltpu.make_async_copy(
            cos.at[0, :, :, lanes(h)],
            density_value.at[h, 1 : CX + 1, PAD : PAD + CY, :],
            sem_c.at[h],
        )

    def copy_e(x, h):
        return pltpu.make_async_copy(
            cos.at[1:NF, x, :, lanes(h)], phases.at[:, h, x + 1, PAD : PAD + CY, :], sem_e.at[x, h]
        )

    def copy_f(x, h):
        return pltpu.make_async_copy(fld.at[:, x, :, lanes(h)], field.at[:, h, x], sem_f.at[x, h])

    inside = slice(8, CY - 8)

    def copy_o(x, h):
        return pltpu.make_async_copy(
            result.at[1:NF, h, x, inside, :], out.at[1:NF, x, inside, lanes(h)], sem_o.at[x, h]
        )

    def copy_d(x, h):
        return pltpu.make_async_copy(
            result.at[0, h, x, inside, :], out.at[0, x, inside, lanes(h)], sem_d.at[x, h]
        )

    for h in BOTH:
        copy_c(h).start()
    for x in range(CX):
        for h in BOTH:
            copy_e(x, h).start()
            copy_f(x, h).start()

    clear_edges(potential)
    clear_edges(density_value)
    for s in range(SLOTS):
        clear_edges(phases.at[s])
    if with_sums:
        sums[...] = jnp.zeros(sums.shape, F32)
    for h in BOTH:
        copy_c(h).wait()
        if not with_sums:
            for edge, y in ((0, PAD), (8, PAD + CY - 1)):
                for k, x in ((0, 1), (1, CX)):
                    density_value[h, x, y : y + 1, :] += corners[h, edge + k : edge + k + 1, :]

    def potential_plane(x):
        for part in range(CY // 8):
            row = PAD + part * 8
            own, total = around(density_value, x, row)
            for h in BOTH:
                potential[h, x + 1, row : row + 8, :] = DT * total[h] - (6.0 * DT) * own[h]

    for x in range(CX):
        potential_plane(x)

    for h in BOTH:
        copy_e(0, h).wait()

    def step_plane(x):
        for h in BOTH if x < CX - 1 else ():
            copy_e(x + 1, h).wait()

        for h in BOTH:
            copy_f(x, h).wait()
        for part in range(CY // 8):
            row = PAD + part * 8
            here = slice(part * 8, part * 8 + 8)
            square = [None] * HALF
            weighted = [None] * HALF
            curved = [None] * HALF
            for s in range(SLOTS):
                for h in BOTH:
                    eta = field[s + 1, h, x, here, :]
                    lam = phases[s, h, x + 1, row : row + 8, :]
                    eta_eta = eta * eta
                    lam_eta = lam * eta
                    cubic = lam_eta * eta
                    square[h] = eta_eta if square[h] is None else square[h] + eta_eta
                    weighted[h] = lam_eta if weighted[h] is None else weighted[h] + lam_eta
                    curved[h] = cubic if curved[h] is None else curved[h] + cubic
            mu, mu_total = around(potential, x, row)
            scale, slope, mu_twelve, linear = [], [], [], []
            for h in BOTH:
                density = field[0, h, x, here, :]
                lam_c = density_value[h, x + 1, row : row + 8, :]
                curvature = 34.0 + density * (192.0 * density - 192.0)
                result[0, h, x, here, :] = (
                    lam_c
                    + mu[h] * (curvature + 6.0)
                    - mu_total[h]
                    - (12.0 * DT) * (curved[h] - weighted[h])
                )
                scale.append((1.0 - 18.0 * DT) + (12.0 * DT) * (density - square[h]))
                slope.append((48.0 * DT) - (24.0 * DT) * density)
                mu_twelve.append(12.0 * mu[h])
                linear.append((24.0 * DT) * weighted[h] + mu_twelve[h])
            for s in range(SLOTS):
                lam, total = around(phases.at[s], x, row)
                for h in BOTH:
                    eta = field[s + 1, h, x, here, :]
                    new = (
                        lam[h] * (scale[h] + slope[h] * eta)
                        + eta * (mu_twelve[h] * eta - linear[h])
                        + DT * total[h]
                    )
                    result[s + 1, h, x, here, :] = new
                    if with_sums:
                        sums[s, h, here, :] += lam[h] + new

        for h in BOTH if 0 < x < CX - 1 else ():
            copy_o(x, h).start()

        for h in BOTH if 1 < x < CX - 2 else ():
            copy_d(x, h).start()

    for x in range(CX):
        step_plane(x)
    for h in BOTH:
        for x in range(1, CX - 1):
            copy_o(x, h).wait()
        for x in range(2, CX - 2):
            copy_d(x, h).wait()


PADDED = jax.ShapeDtypeStruct((HALF, CX + 2, ROWS, LN), F32)
BLOCK = jax.ShapeDtypeStruct((NF, HALF, CX, CY, LN), F32)
SUMS = jax.ShapeDtypeStruct((SLOTS, HALF, CY, LN), F32)
WHOLE = pltpu.HBM((NF, CX, CY, NZ), F32)


def local_step(cos, fld, corners=None):
    with_sums = corners is None
    extra = [SUMS] if with_sums else []
    more = [] if with_sums else [corners]
    return pl.pallas_call(
        functools.partial(local_kernel, with_sums),
        out_shape=[WHOLE, PADDED, BLOCK, BLOCK] + extra,
        in_specs=[HBM, HBM] + [VM] * len(more),
        out_specs=[HBM, VM, VM, VM] + [VM] * len(extra),
        scratch_shapes=[
            pltpu.VMEM((SLOTS, HALF, CX + 2, ROWS, LN), F32),
            pltpu.VMEM((HALF, CX + 2, ROWS, LN), F32),
            pltpu.SemaphoreType.DMA((HALF,)),
            pltpu.SemaphoreType.DMA((CX, HALF)),
            pltpu.SemaphoreType.DMA((CX, HALF)),
            pltpu.SemaphoreType.DMA((CX, HALF)),
            pltpu.SemaphoreType.DMA((CX, HALF)),
        ],
        compiler_params=pltpu.CompilerParams(vmem_limit_bytes=12 << 20),
        cost_estimate=pl.CostEstimate(
            flops=250 * CX * CY * NZ, bytes_accessed=3 * 4 * NF * CX * CY * NZ, transcendentals=0
        ),
        name="local_step",
    )(cos, fld, *more)


def pack_kernel(cos, face_a, face_b, side_a, side_b, tiles, sem_p, sem_t):
    even_x, even_y = even_place()
    out_a = jnp.where(even_x, CX - 1, 0)
    in_a = jnp.where(even_x, CX - 2, 1)
    loads = start_all(
        [
            pltpu.make_async_copy(
                cos.at[:, :, edge * (CY - 8) : edge * (CY - 8) + 8, :], tiles.at[edge], sem_t.at[edge]
            )
            for edge in range(2)
        ]
    )
    copies = []
    for which, face, outer, inner in ((0, face_a, out_a, in_a), (1, face_b, CX - 1 - out_a, CX - 1 - in_a)):
        for h in BOTH:
            phases = face.at[h, 0 : SLOTS * CY, :].reshape(SLOTS, CY, LN)
            parts = (
                (cos.at[1:NF, outer, :, lanes(h)], phases),
                (cos.at[0, outer, :, lanes(h)], face.at[h, SLOTS * CY : SLOTS * CY + CY, :]),
                (cos.at[0, inner, :, lanes(h)], face.at[h, SLOTS * CY + CY : FACE, :]),
            )
            copies += [
                pltpu.make_async_copy(*part, sem_p.at[which, h, k]) for k, part in enumerate(parts)
            ]
    start_all(copies)
    wait_all(loads)
    for h in range(HALF):
        for k in range(SLOTS + 2):
            s = k + 1 if k < SLOTS else 0
            depth = 1 if k == SLOTS + 1 else 0
            low = tiles[0, s, :, depth, lanes(h)]
            high = tiles[1, s, :, 7 - depth, lanes(h)]
            side_a[h, k * CX : (k + 1) * CX, :] = jnp.where(even_y, high, low)
            side_b[h, k * CX : (k + 1) * CX, :] = jnp.where(even_y, low, high)
    wait_all(copies)


def face_message(extra):
    return jax.ShapeDtypeStruct((HALF, FACE + extra, LN), F32)


def side_message(extra):
    return jax.ShapeDtypeStruct((HALF, SIDE + extra, LN), F32)


def pack(cos):
    return pl.pallas_call(
        pack_kernel,
        out_shape=[face_message(0)] * 2 + [side_message(0)] * 2,
        in_specs=[HBM],
        out_specs=[VM] * 4,
        scratch_shapes=[
            pltpu.VMEM((2, NF, CX, 8, NZ), F32),
            pltpu.SemaphoreType.DMA((2, HALF, 3)),
            pltpu.SemaphoreType.DMA((2,)),
        ],
        compiler_params=pltpu.CompilerParams(vmem_limit_bytes=8 << 20),
        name="pack",
    )(cos)


def corner_kernel(sizes, first_a, first_b, order, got_a, got_b, face_a, face_b, *rest):
    del order, got_a, got_b, face_a, face_b
    side_a, side_b, out_a, out_b, corners = rest
    even_x, even_y = even_place()
    row = lax.broadcasted_iota(jnp.int32, (CX, LN), 0)
    face = slice(SLOTS * CX, SLOTS * CX + CX)
    start = SLOTS * CY
    for h in BOTH:
        ends_a = first_a[h, start : start + 1, :], first_a[h, start + CY - 1 : start + CY, :]
        ends_b = first_b[h, start : start + 1, :], first_b[h, start + CY - 1 : start + CY, :]
        fixed = []
        for ref, low_side in ((side_a, ~even_y), (side_b, even_y)):
            end_a = jnp.where(low_side, ends_a[0], ends_a[1])
            end_b = jnp.where(low_side, ends_b[0], ends_b[1])
            at_low = jnp.where(even_x, end_b, end_a)
            at_high = jnp.where(even_x, end_a, end_b)
            term = jnp.where(row == 0, at_low, jnp.where(row == CX - 1, at_high, 0.0))
            exists = jnp.where(low_side, *has_neighbours("gy", sizes[1]))
            value = ref[h, face, :] - (2.0 * DT * exists) * term
            ref[h, face, :] = value
            fixed.append(value)
        low = jnp.where(even_y, fixed[1], fixed[0])
        high = jnp.where(even_y, fixed[0], fixed[1])
        beyond_a, beyond_b = side_a[h, SIDE : SIDE + 8, :], side_b[h, SIDE : SIDE + 8, :]
        beyond_low = (-2.0 * DT) * jnp.where(even_y, beyond_b, beyond_a)
        beyond_high = (-2.0 * DT) * jnp.where(even_y, beyond_a, beyond_b)
        corners[h, 0:8, :] = beyond_low
        corners[h, 8:16, :] = beyond_high
        at_low = jnp.where(row == 0, low[0:1, :], high[0:1, :])
        at_high = jnp.where(row == 0, low[CX - 1 : CX, :], high[CX - 1 : CX, :])
        for ref, high_face in ((out_a, even_x), (out_b, ~even_x)):
            ref[h, FACE : FACE + 8, :] = jnp.where(high_face, at_high, at_low)
            ref[h, start : start + 1, :] += jnp.where(high_face, beyond_low[1:2, :], beyond_low[0:1, :])
            ref[h, start + CY - 1 : start + CY, :] += jnp.where(
                high_face, beyond_high[1:2, :], beyond_high[0:1, :]
            )


CORNERS = jax.ShapeDtypeStruct((HALF, 16, LN), F32)


def corner(sizes, first, order, got, faces):
    return pl.pallas_call(
        functools.partial(corner_kernel, sizes),
        out_shape=[side_message(EXTRA)] * 2 + [face_message(EXTRA)] * 2 + [CORNERS],
        in_specs=[VM, VM, HBM] + [VM] * 4,
        out_specs=[VM] * 5,
        input_output_aliases={3: 0, 4: 1, 5: 2, 6: 3},
        compiler_params=pltpu.CompilerParams(vmem_limit_bytes=LIMIT),
        name="corner",
    )(*first, order, *got, *faces)


def grain_rows(groups, grains, sums, rows):
    rows[...] = jnp.zeros(rows.shape, F32)
    row = lax.broadcasted_iota(jnp.int32, (GRAIN_DEV, LN), 0)
    for t in range(CY // 8):
        for s in range(SLOTS):
            grain = grains[0, t, s]
            start = pl.multiple_of(grain // (GRAIN_DEV * groups) * GRAIN_DEV, GRAIN_DEV)
            chosen = row == grain % GRAIN_DEV
            for h in range(HALF):
                total = DT * jnp.sum(sums[s, h, t * 8 : t * 8 + 8, :], axis=0, keepdims=True)
                rows[pl.ds(start, GRAIN_DEV), lanes(h)] += jnp.where(chosen, total, 0.0)


def fix_kernel(sizes, stage, *refs):
    sums = None
    if stage == "early":
        value, field, got_fa, got_fb, got_sa, got_sb, _, _, work, sums, side_a, side_b, edge = refs
        spans = (slice(0, 8), slice(CY - 8, CY))
    elif stage == "late":
        grains, value, field, got_fa, got_fb, _, _, _, work, out, sums, face_a, face_b, rows, edge, sem = refs
        spans = (slice(8, CY - 8),)
    else:
        value, field, got_fa, got_fb, got_sa, got_sb, _, _, work, out, edge, sem = refs
        spans = (slice(0, CY),)
    even_x, even_y = even_place()
    near_x = has_neighbours("gx", sizes[0])
    near_y = has_neighbours("gy", sizes[1])
    stores = []

    def store(*where):
        s, x, y = where
        for h in BOTH if stage != "early" else ():
            stores.append(
                pltpu.make_async_copy(work.at[s, h, x, y, :], out.at[s, x, y, lanes(h)], sem.at[len(stores)])
            )
            stores[-1].start()

    row = lax.broadcasted_iota(jnp.int32, (CX, LN), 0)
    for y, inner, present in ((0, 1, near_y[0]), (CY - 1, CY - 2, near_y[1])):
        near = slice(0, 8) if y == 0 else slice(CY - 8, CY)
        if stage == "late":
            store(slice(1, NF), slice(1, CX - 1), near)
            store(0, slice(2, CX - 2), near)
            continue

        def got(h, start):
            a = got_sa[h, start : start + CX, :]
            b = got_sb[h, start : start + CX, :]
            return jnp.where(even_y, b, a) if y == 0 else jnp.where(even_y, a, b)

        exists = present * DT
        delta = [DT * got(h, SLOTS * CX) for h in BOTH]
        along_z = z_sum(*delta)
        twelve = []
        for h in BOTH:
            d = delta[h]
            along_x = jnp.where(row == 0, 0.0, pltpu.roll(d, 1, 0)) + jnp.where(
                row == CX - 1, 0.0, pltpu.roll(d, CX - 1, 0)
            )
            total = along_z[h] + along_x - 6.0 * d
            density = field[0, h, :, y, :]
            curvature = 34.0 + density * (192.0 * density - 192.0)
            work[0, h, :, y, :] = work[0, h, :, y, :] + (
                d * curvature
                - 2.0 * total
                - DT * got(h, (SLOTS + 1) * CX)
                - exists * value[h, 1 : CX + 1, PAD + y, :]
            )
            work[0, h, :, inner, :] = work[0, h, :, inner, :] - d
            twelve.append(12.0 * d)
        for s in range(1, NF):
            for h in BOTH:
                eta = field[s, h, :, y, :]
                change = DT * got(h, (s - 1) * CX) + twelve[h] * (eta * eta - eta)
                work[s, h, :, y, :] = work[s, h, :, y, :] + change
                if sums is not None:
                    sums[s - 1, h, y : y + 1, :] += jnp.sum(change, axis=0, keepdims=True)
        store(slice(1, NF), slice(1, CX - 1), near)
        store(0, slice(2, CX - 2), near)

    for x, inner, present in ((0, 1, near_x[0]), (CX - 1, CX - 2, near_x[1])):

        def got(h, start, size):
            a = got_fa[h, start : start + size, :]
            b = got_fb[h, start : start + size, :]
            return jnp.where(even_x, b, a) if x == 0 else jnp.where(even_x, a, b)

        exists = present * DT
        delta = []
        for h in BOTH:
            d = DT * got(h, SLOTS * CY, CY)
            delta.append(d)
            edge[h, 8 : 8 + CY, :] = d
            if sums is not None:
                edge[h, 0:8, :] = jnp.zeros((8, LN), F32)
                edge[h, 8 + CY : 16 + CY, :] = jnp.zeros((8, LN), F32)
            else:
                ends = DT * got(h, FACE, 8)
                edge[h, 7:8, :] = ends[0:1, :]
                edge[h, 8 + CY : 9 + CY, :] = ends[1:2, :]
        for span in spans:
            size = span.stop - span.start
            part = [d[span] for d in delta]
            along_z = z_sum(*part)
            twelve = []
            for h in BOTH:
                above = edge[h, 9 + span.start : 9 + span.stop, :]
                below = edge[h, 7 + span.start : 7 + span.stop, :]
                total = along_z[h] + above + below - 6.0 * part[h]
                density = field[0, h, x, span, :]
                curvature = 34.0 + density * (192.0 * density - 192.0)
                work[0, h, x, span, :] += (
                    part[h] * curvature
                    - 2.0 * total
                    - DT * got(h, (SLOTS + 1) * CY + span.start, size)
                    - exists * value[h, x + 1, PAD + span.start : PAD + span.stop, :]
                )
                work[0, h, inner, span, :] -= part[h]
                twelve.append(12.0 * part[h])
            for s in range(1, NF):
                for h in BOTH:
                    eta = field[s, h, x, span, :]
                    change = DT * got(h, (s - 1) * CY + span.start, size) + twelve[h] * (eta * eta - eta)
                    work[s, h, x, span, :] += change
                    if sums is not None:
                        sums[s - 1, h, span, :] += change
        store(slice(0, NF), x, slice(0, CY))
        store(0, inner, slice(0, CY))

    for h in BOTH:
        for k in range(SLOTS + 2):
            s = k + 1 if k < SLOTS else 0
            depth = 1 if k == SLOTS + 1 else 0
            if stage == "late":
                low, high = (work[s, h, x] for x in (depth, CX - 1 - depth))
                face_a[h, k * CY : (k + 1) * CY, :] = jnp.where(even_x, high, low)
                face_b[h, k * CY : (k + 1) * CY, :] = jnp.where(even_x, low, high)
            if stage == "early":
                low, high = (work[s, h, :, y, :] for y in (depth, CY - 1 - depth))
                side_a[h, k * CX : (k + 1) * CX, :] = jnp.where(even_y, high, low)
                side_b[h, k * CX : (k + 1) * CX, :] = jnp.where(even_y, low, high)
        if stage == "early":
            start = SLOTS * CY
            ends = []
            for at in (start, start + CY - 1):
                a, b = got_fa[h, at : at + 1, :], got_fb[h, at : at + 1, :]
                at_low, at_high = jnp.where(even_x, b, a), jnp.where(even_x, a, b)
                ends.append(jnp.where(row == 0, at_low, at_high))
            side_a[h, SIDE : SIDE + 8, :] = jnp.where(even_y, ends[1], ends[0])
            side_b[h, SIDE : SIDE + 8, :] = jnp.where(even_y, ends[0], ends[1])
    if stage == "late":
        grain_rows(sizes[1], grains, sums, rows)
    wait_all(stores)


EDGE = pltpu.VMEM((HALF, ROWS, LN), F32)
STORES = pltpu.SemaphoreType.DMA((16,))


def fix_early(sizes, value, field, got_faces, got_sides, base, sums):
    return pl.pallas_call(
        functools.partial(fix_kernel, sizes, "early"),
        out_shape=[BLOCK, SUMS] + [side_message(EXTRA)] * 2,
        in_specs=[VM] * 8,
        out_specs=[VM] * 4,
        scratch_shapes=[EDGE],
        input_output_aliases={6: 0, 7: 1},
        compiler_params=pltpu.CompilerParams(vmem_limit_bytes=LIMIT),
        name="fix_early",
    )(value, field, *got_faces, *got_sides, base, sums)


def fix_late(sizes, slot_grain, value, field, got_faces, base, out, sums):
    rows = jax.ShapeDtypeStruct((sizes[0] * GRAIN_DEV, NZ), F32)
    return pl.pallas_call(
        functools.partial(fix_kernel, sizes, "late"),
        out_shape=[BLOCK, WHOLE, SUMS] + [face_message(EXTRA)] * 2 + [rows],
        in_specs=[SM] + [VM] * 5 + [HBM, VM],
        out_specs=[VM, HBM] + [VM] * 4,
        scratch_shapes=[EDGE, STORES],
        input_output_aliases={5: 0, 6: 1, 7: 2},
        compiler_params=pltpu.CompilerParams(vmem_limit_bytes=LIMIT),
        name="fix_late",
    )(slot_grain, value, field, *got_faces, base, out, sums)


def fix_whole(sizes, value, field, got_faces, got_sides, base, out):
    return pl.pallas_call(
        functools.partial(fix_kernel, sizes, "whole"),
        out_shape=[BLOCK, WHOLE],
        in_specs=[VM] * 7 + [HBM],
        out_specs=[VM, HBM],
        scratch_shapes=[EDGE, STORES],
        input_output_aliases={6: 0, 7: 1},
        compiler_params=pltpu.CompilerParams(vmem_limit_bytes=LIMIT),
        name="fix_whole",
    )(value, field, *got_faces, *got_sides, base, out)[1]


def swaps(axis, count, first, second):
    near = [(i, i ^ 1) for i in range(count)]
    far = [(i, ((i + 1) ^ 1) - 1) for i in range(1, count - 1)]
    return lax.ppermute(first, axis, near), lax.ppermute(second, axis, far)


def shards(n_gx, n_gy, cotangent, fields_one, fields_zero, slot_grain):
    sizes = n_gx, n_gy
    cotangent, fields_one, fields_zero = (
        pltpu.with_memory_space_constraint(array, pltpu.HBM)
        for array in (cotangent, fields_one, fields_zero)
    )
    face_a, face_b, side_a, side_b = pack(cotangent)
    first_faces = swaps("gx", n_gx, face_a, face_b)
    got_sides = swaps("gy", n_gy, side_a, side_b)
    out, value, field, base, sums = local_step(cotangent, fields_one)
    base, sums, side_a, side_b = fix_early(sizes, value, field, first_faces, got_sides, base, sums)

    got_sides = swaps("gy", n_gy, side_a, side_b)
    _, costate, _, face_a, face_b, rows = fix_late(
        sizes, slot_grain, value, field, first_faces, base, out, sums
    )
    side_a, side_b, face_a, face_b, corners = corner(
        sizes, first_faces, rows, got_sides, (face_a, face_b)
    )
    got_faces = swaps("gx", n_gx, face_a, face_b)
    got_rows = lax.all_to_all(
        rows.reshape(n_gx, GRAIN_DEV, NZ), "gx", split_axis=0, concat_axis=0, tiled=True
    )
    costate = pltpu.with_memory_space_constraint(costate, pltpu.HBM)
    out, value, field, base = local_step(costate, fields_zero, corners)
    adjoint = fix_whole(sizes, value, field, got_faces, (side_a, side_b), base, out)
    got_rows, adjoint = lax.optimization_barrier((got_rows, adjoint))
    grain_grad = jnp.sum(got_rows.reshape(n_gx, GRAIN_DEV, NZ), axis=0)
    return adjoint, grain_grad


def solution(mesh):
    placed = (
        P(None, "gx", "gy", None),
        P(None, "gx", "gy", None),
        P(None, "gx", "gy", None),
        P("gx", "gy", None),
    )
    return jax.shard_map(
        functools.partial(shards, mesh.shape["gx"], mesh.shape["gy"]),
        mesh=mesh,
        in_specs=placed,
        out_specs=(P(None, "gx", "gy", None), P(("gx", "gy"), None)),
        check_vma=False,
    )
```

```python
import functools

import jax
import jax.numpy as jnp
from jax import lax
from jax.experimental import pallas as pl
from jax.experimental.pallas import tpu as pltpu
from jax.sharding import PartitionSpec as P

DT = 0.05
SLOTS = 8
NF = SLOTS + 1
CX, CY, NZ = 8, 64, 256
LN = 128
HALF = NZ // LN
GRAIN_DEV = 8
PAD = 8
ROWS = CY + 2 * PAD
FACE = (SLOTS + 2) * CY
SIDE = (SLOTS + 2) * CX
EXTRA = 8
F32 = jnp.float32
BOTH = range(HALF)
LIMIT = 4 << 20
HBM = pl.BlockSpec(memory_space=pltpu.HBM)
VM = pl.BlockSpec(memory_space=pltpu.VMEM)
SM = pl.BlockSpec(memory_space=pltpu.SMEM)


def lanes(half):
    return slice(half * LN, (half + 1) * LN)


def z_sum(first, second):
    lane = lax.broadcasted_iota(jnp.int32, first.shape, first.ndim - 1)
    axis = first.ndim - 1
    low, high = lane == 0, lane == LN - 1
    from_low = pltpu.roll(first, 1, axis)
    from_high = pltpu.roll(second, LN - 1, axis)
    left = jnp.where(low, 0.0, from_low), jnp.where(low, from_low, pltpu.roll(second, 1, axis))
    right = jnp.where(high, from_high, pltpu.roll(first, LN - 1, axis)), jnp.where(high, 0.0, from_high)
    return left[0] + right[0], left[1] + right[1]


def even_place():
    return lax.rem(lax.axis_index("gx"), 2) == 1, lax.rem(lax.axis_index("gy"), 2) == 1


def has_neighbours(axis, count):
    index = lax.axis_index(axis)
    return tuple(jnp.where(beside, 1.0, 0.0) for beside in (index > 0, index < count - 1))


def start_all(copies):
    for copy in copies:
        copy.start()
    return copies


def wait_all(copies):
    for copy in copies:
        copy.wait()


def around(ref, x, row):
    own = [ref[h, x + 1, row : row + 8, :] for h in BOTH]
    along_z = z_sum(*own)
    total = [
        (ref[h, x, row : row + 8, :] + ref[h, x + 2, row : row + 8, :])
        + (ref[h, x + 1, row - 1 : row + 7, :] + ref[h, x + 1, row + 1 : row + 9, :])
        + along_z[h]
        for h in BOTH
    ]
    return own, total


def clear_edges(ref):
    tile = jnp.zeros((8, LN), F32)
    plane = jnp.zeros((CY, LN), F32)
    for h in BOTH:
        ref[h, 0, PAD : PAD + CY, :] = plane
        ref[h, CX + 1, PAD : PAD + CY, :] = plane
        for x in range(1, CX + 1):
            ref[h, x, 0:PAD, :] = tile
            ref[h, x, PAD + CY : ROWS, :] = tile


def local_kernel(with_sums, cos, fld, *rest):
    if with_sums:
        out, density_value, field, result, sums, *rest = rest
    else:
        corners, out, density_value, field, result, *rest = rest
    phases, potential, sem_c, sem_e, sem_f, sem_o, sem_d = rest

    def copy_c(h):
        return pltpu.make_async_copy(
            cos.at[0, :, :, lanes(h)],
            density_value.at[h, 1 : CX + 1, PAD : PAD + CY, :],
            sem_c.at[h],
        )

    def copy_e(x, h):
        return pltpu.make_async_copy(
            cos.at[1:NF, x, :, lanes(h)], phases.at[:, h, x + 1, PAD : PAD + CY, :], sem_e.at[x, h]
        )

    def copy_f(x, h):
        return pltpu.make_async_copy(fld.at[:, x, :, lanes(h)], field.at[:, h, x], sem_f.at[x, h])

    inside = slice(8, CY - 8)

    def copy_o(x, h):
        return pltpu.make_async_copy(
            result.at[1:NF, h, x, inside, :], out.at[1:NF, x, inside, lanes(h)], sem_o.at[x, h]
        )

    def copy_d(x, h):
        return pltpu.make_async_copy(
            result.at[0, h, x, inside, :], out.at[0, x, inside, lanes(h)], sem_d.at[x, h]
        )

    for h in BOTH:
        copy_c(h).start()
    for x in range(CX):
        for h in BOTH:
            copy_e(x, h).start()
            copy_f(x, h).start()

    clear_edges(potential)
    clear_edges(density_value)
    for s in range(SLOTS):
        clear_edges(phases.at[s])
    if with_sums:
        sums[...] = jnp.zeros(sums.shape, F32)
    for h in BOTH:
        copy_c(h).wait()
        if not with_sums:
            for edge, y in ((0, PAD), (8, PAD + CY - 1)):
                for k, x in ((0, 1), (1, CX)):
                    density_value[h, x, y : y + 1, :] += corners[h, edge + k : edge + k + 1, :]

    def potential_plane(x):
        for part in range(CY // 8):
            row = PAD + part * 8
            own, total = around(density_value, x, row)
            for h in BOTH:
                potential[h, x + 1, row : row + 8, :] = DT * total[h] - (6.0 * DT) * own[h]

    for x in range(CX):
        potential_plane(x)

    for h in BOTH:
        copy_e(0, h).wait()

    def step_plane(x):
        for h in BOTH if x < CX - 1 else ():
            copy_e(x + 1, h).wait()

        for h in BOTH:
            copy_f(x, h).wait()
        for part in range(CY // 8):
            row = PAD + part * 8
            here = slice(part * 8, part * 8 + 8)
            square = [None] * HALF
            weighted = [None] * HALF
            curved = [None] * HALF
            for s in range(SLOTS):
                for h in BOTH:
                    eta = field[s + 1, h, x, here, :]
                    lam = phases[s, h, x + 1, row : row + 8, :]
                    eta_eta = eta * eta
                    lam_eta = lam * eta
                    cubic = lam_eta * eta
                    square[h] = eta_eta if square[h] is None else square[h] + eta_eta
                    weighted[h] = lam_eta if weighted[h] is None else weighted[h] + lam_eta
                    curved[h] = cubic if curved[h] is None else curved[h] + cubic
            mu, mu_total = around(potential, x, row)
            scale, slope, mu_twelve, linear = [], [], [], []
            for h in BOTH:
                density = field[0, h, x, here, :]
                lam_c = density_value[h, x + 1, row : row + 8, :]
                curvature = 34.0 + density * (192.0 * density - 192.0)
                result[0, h, x, here, :] = (
                    lam_c
                    + mu[h] * (curvature + 6.0)
                    - mu_total[h]
                    - (12.0 * DT) * (curved[h] - weighted[h])
                )
                scale.append((1.0 - 18.0 * DT) + (12.0 * DT) * (density - square[h]))
                slope.append((48.0 * DT) - (24.0 * DT) * density)
                mu_twelve.append(12.0 * mu[h])
                linear.append((24.0 * DT) * weighted[h] + mu_twelve[h])
            for s in range(SLOTS):
                lam, total = around(phases.at[s], x, row)
                for h in BOTH:
                    eta = field[s + 1, h, x, here, :]
                    new = (
                        lam[h] * (scale[h] + slope[h] * eta)
                        + eta * (mu_twelve[h] * eta - linear[h])
                        + DT * total[h]
                    )
                    result[s + 1, h, x, here, :] = new
                    if with_sums:
                        sums[s, h, here, :] += lam[h] + new

        for h in BOTH if 0 < x < CX - 1 else ():
            copy_o(x, h).start()

        for h in BOTH if 1 < x < CX - 2 else ():
            copy_d(x, h).start()

    for x in range(CX):
        step_plane(x)
    for h in BOTH:
        for x in range(1, CX - 1):
            copy_o(x, h).wait()
        for x in range(2, CX - 2):
            copy_d(x, h).wait()


PADDED = jax.ShapeDtypeStruct((HALF, CX + 2, ROWS, LN), F32)
BLOCK = jax.ShapeDtypeStruct((NF, HALF, CX, CY, LN), F32)
SUMS = jax.ShapeDtypeStruct((SLOTS, HALF, CY, LN), F32)
WHOLE = pltpu.HBM((NF, CX, CY, NZ), F32)


def local_step(cos, fld, corners=None):
    with_sums = corners is None
    extra = [SUMS] if with_sums else []
    more = [] if with_sums else [corners]
    return pl.pallas_call(
        functools.partial(local_kernel, with_sums),
        out_shape=[WHOLE, PADDED, BLOCK, BLOCK] + extra,
        in_specs=[HBM, HBM] + [VM] * len(more),
        out_specs=[HBM, VM, VM, VM] + [VM] * len(extra),
        scratch_shapes=[
            pltpu.VMEM((SLOTS, HALF, CX + 2, ROWS, LN), F32),
            pltpu.VMEM((HALF, CX + 2, ROWS, LN), F32),
            pltpu.SemaphoreType.DMA((HALF,)),
            pltpu.SemaphoreType.DMA((CX, HALF)),
            pltpu.SemaphoreType.DMA((CX, HALF)),
            pltpu.SemaphoreType.DMA((CX, HALF)),
            pltpu.SemaphoreType.DMA((CX, HALF)),
        ],
        compiler_params=pltpu.CompilerParams(vmem_limit_bytes=12 << 20),
        cost_estimate=pl.CostEstimate(
            flops=250 * CX * CY * NZ, bytes_accessed=3 * 4 * NF * CX * CY * NZ, transcendentals=0
        ),
        name="local_step",
    )(cos, fld, *more)


def pack_kernel(cos, face_a, face_b, side_a, side_b, tiles, sem_p, sem_t):
    even_x, even_y = even_place()
    out_a = jnp.where(even_x, CX - 1, 0)
    in_a = jnp.where(even_x, CX - 2, 1)
    loads = start_all(
        [
            pltpu.make_async_copy(
                cos.at[:, :, edge * (CY - 8) : edge * (CY - 8) + 8, :], tiles.at[edge], sem_t.at[edge]
            )
            for edge in range(2)
        ]
    )
    copies = []
    for which, face, outer, inner in ((0, face_a, out_a, in_a), (1, face_b, CX - 1 - out_a, CX - 1 - in_a)):
        for h in BOTH:
            phases = face.at[h, 0 : SLOTS * CY, :].reshape(SLOTS, CY, LN)
            parts = (
                (cos.at[1:NF, outer, :, lanes(h)], phases),
                (cos.at[0, outer, :, lanes(h)], face.at[h, SLOTS * CY : SLOTS * CY + CY, :]),
                (cos.at[0, inner, :, lanes(h)], face.at[h, SLOTS * CY + CY : FACE, :]),
            )
            copies += [
                pltpu.make_async_copy(*part, sem_p.at[which, h, k]) for k, part in enumerate(parts)
            ]
    start_all(copies)
    wait_all(loads)
    for h in range(HALF):
        for k in range(SLOTS + 2):
            s = k + 1 if k < SLOTS else 0
            depth = 1 if k == SLOTS + 1 else 0
            low = tiles[0, s, :, depth, lanes(h)]
            high = tiles[1, s, :, 7 - depth, lanes(h)]
            side_a[h, k * CX : (k + 1) * CX, :] = jnp.where(even_y, high, low)
            side_b[h, k * CX : (k + 1) * CX, :] = jnp.where(even_y, low, high)
    wait_all(copies)


def face_message(extra):
    return jax.ShapeDtypeStruct((HALF, FACE + extra, LN), F32)


def side_message(extra):
    return jax.ShapeDtypeStruct((HALF, SIDE + extra, LN), F32)


def pack(cos):
    return pl.pallas_call(
        pack_kernel,
        out_shape=[face_message(0)] * 2 + [side_message(0)] * 2,
        in_specs=[HBM],
        out_specs=[VM] * 4,
        scratch_shapes=[
            pltpu.VMEM((2, NF, CX, 8, NZ), F32),
            pltpu.SemaphoreType.DMA((2, HALF, 3)),
            pltpu.SemaphoreType.DMA((2,)),
        ],
        compiler_params=pltpu.CompilerParams(vmem_limit_bytes=8 << 20),
        name="pack",
    )(cos)


def corner_kernel(sizes, first_a, first_b, order, got_a, got_b, face_a, face_b, *rest):
    del order, got_a, got_b, face_a, face_b
    side_a, side_b, out_a, out_b, corners = rest
    even_x, even_y = even_place()
    row = lax.broadcasted_iota(jnp.int32, (CX, LN), 0)
    face = slice(SLOTS * CX, SLOTS * CX + CX)
    start = SLOTS * CY
    for h in BOTH:
        ends_a = first_a[h, start : start + 1, :], first_a[h, start + CY - 1 : start + CY, :]
        ends_b = first_b[h, start : start + 1, :], first_b[h, start + CY - 1 : start + CY, :]
        fixed = []
        for ref, low_side in ((side_a, ~even_y), (side_b, even_y)):
            end_a = jnp.where(low_side, ends_a[0], ends_a[1])
            end_b = jnp.where(low_side, ends_b[0], ends_b[1])
            at_low = jnp.where(even_x, end_b, end_a)
            at_high = jnp.where(even_x, end_a, end_b)
            term = jnp.where(row == 0, at_low, jnp.where(row == CX - 1, at_high, 0.0))
            exists = jnp.where(low_side, *has_neighbours("gy", sizes[1]))
            value = ref[h, face, :] - (2.0 * DT * exists) * term
            ref[h, face, :] = value
            fixed.append(value)
        low = jnp.where(even_y, fixed[1], fixed[0])
        high = jnp.where(even_y, fixed[0], fixed[1])
        beyond_a, beyond_b = side_a[h, SIDE : SIDE + 8, :], side_b[h, SIDE : SIDE + 8, :]
        beyond_low = (-2.0 * DT) * jnp.where(even_y, beyond_b, beyond_a)
        beyond_high = (-2.0 * DT) * jnp.where(even_y, beyond_a, beyond_b)
        corners[h, 0:8, :] = beyond_low
        corners[h, 8:16, :] = beyond_high
        at_low = jnp.where(row == 0, low[0:1, :], high[0:1, :])
        at_high = jnp.where(row == 0, low[CX - 1 : CX, :], high[CX - 1 : CX, :])
        for ref, high_face in ((out_a, even_x), (out_b, ~even_x)):
            ref[h, FACE : FACE + 8, :] = jnp.where(high_face, at_high, at_low)
            ref[h, start : start + 1, :] += jnp.where(high_face, beyond_low[1:2, :], beyond_low[0:1, :])
            ref[h, start + CY - 1 : start + CY, :] += jnp.where(
                high_face, beyond_high[1:2, :], beyond_high[0:1, :]
            )


CORNERS = jax.ShapeDtypeStruct((HALF, 16, LN), F32)


def corner(sizes, first, order, got, faces):
    return pl.pallas_call(
        functools.partial(corner_kernel, sizes),
        out_shape=[side_message(EXTRA)] * 2 + [face_message(EXTRA)] * 2 + [CORNERS],
        in_specs=[VM, VM, HBM] + [VM] * 4,
        out_specs=[VM] * 5,
        input_output_aliases={3: 0, 4: 1, 5: 2, 6: 3},
        compiler_params=pltpu.CompilerParams(vmem_limit_bytes=LIMIT),
        name="corner",
    )(*first, order, *got, *faces)


def grain_rows(groups, grains, sums, rows):
    rows[...] = jnp.zeros(rows.shape, F32)
    row = lax.broadcasted_iota(jnp.int32, (GRAIN_DEV, LN), 0)
    for t in range(CY // 8):
        for s in range(SLOTS):
            grain = grains[0, t, s]
            start = pl.multiple_of(grain // (GRAIN_DEV * groups) * GRAIN_DEV, GRAIN_DEV)
            chosen = row == grain % GRAIN_DEV
            for h in range(HALF):
                total = DT * jnp.sum(sums[s, h, t * 8 : t * 8 + 8, :], axis=0, keepdims=True)
                rows[pl.ds(start, GRAIN_DEV), lanes(h)] += jnp.where(chosen, total, 0.0)


def fix_kernel(sizes, stage, *refs):
    sums = None
    if stage == "early":
        value, field, got_fa, got_fb, got_sa, got_sb, _, _, work, sums, side_a, side_b, edge = refs
        spans = (slice(0, 8), slice(CY - 8, CY))
    elif stage == "late":
        grains, value, field, got_fa, got_fb, _, _, _, work, out, sums, face_a, face_b, rows, edge, sem = refs
        spans = (slice(8, CY - 8),)
    else:
        value, field, got_fa, got_fb, got_sa, got_sb, _, _, work, out, edge, sem = refs
        spans = (slice(0, CY),)
    even_x, even_y = even_place()
    near_x = has_neighbours("gx", sizes[0])
    near_y = has_neighbours("gy", sizes[1])
    stores = []

    def store(*where):
        s, x, y = where
        for h in BOTH if stage != "early" else ():
            stores.append(
                pltpu.make_async_copy(work.at[s, h, x, y, :], out.at[s, x, y, lanes(h)], sem.at[len(stores)])
            )
            stores[-1].start()

    row = lax.broadcasted_iota(jnp.int32, (CX, LN), 0)
    for y, inner, present in ((0, 1, near_y[0]), (CY - 1, CY - 2, near_y[1])):
        near = slice(0, 8) if y == 0 else slice(CY - 8, CY)
        if stage == "late":
            store(slice(1, NF), slice(1, CX - 1), near)
            store(0, slice(2, CX - 2), near)
            continue

        def got(h, start):
            a = got_sa[h, start : start + CX, :]
            b = got_sb[h, start : start + CX, :]
            return jnp.where(even_y, b, a) if y == 0 else jnp.where(even_y, a, b)

        exists = present * DT
        delta = [DT * got(h, SLOTS * CX) for h in BOTH]
        along_z = z_sum(*delta)
        twelve = []
        for h in BOTH:
            d = delta[h]
            along_x = jnp.where(row == 0, 0.0, pltpu.roll(d, 1, 0)) + jnp.where(
                row == CX - 1, 0.0, pltpu.roll(d, CX - 1, 0)
            )
            total = along_z[h] + along_x - 6.0 * d
            density = field[0, h, :, y, :]
            curvature = 34.0 + density * (192.0 * density - 192.0)
            work[0, h, :, y, :] = work[0, h, :, y, :] + (
                d * curvature
                - 2.0 * total
                - DT * got(h, (SLOTS + 1) * CX)
                - exists * value[h, 1 : CX + 1, PAD + y, :]
            )
            work[0, h, :, inner, :] = work[0, h, :, inner, :] - d
            twelve.append(12.0 * d)
        for s in range(1, NF):
            for h in BOTH:
                eta = field[s, h, :, y, :]
                change = DT * got(h, (s - 1) * CX) + twelve[h] * (eta * eta - eta)
                work[s, h, :, y, :] = work[s, h, :, y, :] + change
                if sums is not None:
                    sums[s - 1, h, y : y + 1, :] += jnp.sum(change, axis=0, keepdims=True)
        store(slice(1, NF), slice(1, CX - 1), near)
        store(0, slice(2, CX - 2), near)

    for x, inner, present in ((0, 1, near_x[0]), (CX - 1, CX - 2, near_x[1])):

        def got(h, start, size):
            a = got_fa[h, start : start + size, :]
            b = got_fb[h, start : start + size, :]
            return jnp.where(even_x, b, a) if x == 0 else jnp.where(even_x, a, b)

        exists = present * DT
        delta = []
        for h in BOTH:
            d = DT * got(h, SLOTS * CY, CY)
            delta.append(d)
            edge[h, 8 : 8 + CY, :] = d
            if sums is not None:
                edge[h, 0:8, :] = jnp.zeros((8, LN), F32)
                edge[h, 8 + CY : 16 + CY, :] = jnp.zeros((8, LN), F32)
            else:
                ends = DT * got(h, FACE, 8)
                edge[h, 7:8, :] = ends[0:1, :]
                edge[h, 8 + CY : 9 + CY, :] = ends[1:2, :]
        for span in spans:
            size = span.stop - span.start
            part = [d[span] for d in delta]
            along_z = z_sum(*part)
            twelve = []
            for h in BOTH:
                above = edge[h, 9 + span.start : 9 + span.stop, :]
                below = edge[h, 7 + span.start : 7 + span.stop, :]
                total = along_z[h] + above + below - 6.0 * part[h]
                density = field[0, h, x, span, :]
                curvature = 34.0 + density * (192.0 * density - 192.0)
                work[0, h, x, span, :] += (
                    part[h] * curvature
                    - 2.0 * total
                    - DT * got(h, (SLOTS + 1) * CY + span.start, size)
                    - exists * value[h, x + 1, PAD + span.start : PAD + span.stop, :]
                )
                work[0, h, inner, span, :] -= part[h]
                twelve.append(12.0 * part[h])
            store(0, x, slice(0, CY))
            store(0, inner, slice(0, CY))
            for s in range(1, NF):
                for h in BOTH:
                    eta = field[s, h, x, span, :]
                    change = DT * got(h, (s - 1) * CY + span.start, size) + twelve[h] * (eta * eta - eta)
                    work[s, h, x, span, :] += change
                    if sums is not None:
                        sums[s - 1, h, span, :] += change
                if s % 4 == 0:
                    store(slice(s - 3, s + 1), x, slice(0, CY))

    for h in BOTH:
        for k in range(SLOTS + 2):
            s = k + 1 if k < SLOTS else 0
            depth = 1 if k == SLOTS + 1 else 0
            if stage == "late":
                low, high = (work[s, h, x] for x in (depth, CX - 1 - depth))
                face_a[h, k * CY : (k + 1) * CY, :] = jnp.where(even_x, high, low)
                face_b[h, k * CY : (k + 1) * CY, :] = jnp.where(even_x, low, high)
            if stage == "early":
                low, high = (work[s, h, :, y, :] for y in (depth, CY - 1 - depth))
                side_a[h, k * CX : (k + 1) * CX, :] = jnp.where(even_y, high, low)
                side_b[h, k * CX : (k + 1) * CX, :] = jnp.where(even_y, low, high)
        if stage == "early":
            start = SLOTS * CY
            ends = []
            for at in (start, start + CY - 1):
                a, b = got_fa[h, at : at + 1, :], got_fb[h, at : at + 1, :]
                at_low, at_high = jnp.where(even_x, b, a), jnp.where(even_x, a, b)
                ends.append(jnp.where(row == 0, at_low, at_high))
            side_a[h, SIDE : SIDE + 8, :] = jnp.where(even_y, ends[1], ends[0])
            side_b[h, SIDE : SIDE + 8, :] = jnp.where(even_y, ends[0], ends[1])
    if stage == "late":
        grain_rows(sizes[1], grains, sums, rows)
    wait_all(stores)


EDGE = pltpu.VMEM((HALF, ROWS, LN), F32)
STORES = pltpu.SemaphoreType.DMA((24,))


def fix_early(sizes, value, field, got_faces, got_sides, base, sums):
    return pl.pallas_call(
        functools.partial(fix_kernel, sizes, "early"),
        out_shape=[BLOCK, SUMS] + [side_message(EXTRA)] * 2,
        in_specs=[VM] * 8,
        out_specs=[VM] * 4,
        scratch_shapes=[EDGE],
        input_output_aliases={6: 0, 7: 1},
        compiler_params=pltpu.CompilerParams(vmem_limit_bytes=LIMIT),
        name="fix_early",
    )(value, field, *got_faces, *got_sides, base, sums)


def fix_late(sizes, slot_grain, value, field, got_faces, base, out, sums):
    rows = jax.ShapeDtypeStruct((sizes[0] * GRAIN_DEV, NZ), F32)
    return pl.pallas_call(
        functools.partial(fix_kernel, sizes, "late"),
        out_shape=[BLOCK, WHOLE, SUMS] + [face_message(EXTRA)] * 2 + [rows],
        in_specs=[SM] + [VM] * 5 + [HBM, VM],
        out_specs=[VM, HBM] + [VM] * 4,
        scratch_shapes=[EDGE, STORES],
        input_output_aliases={5: 0, 6: 1, 7: 2},
        compiler_params=pltpu.CompilerParams(vmem_limit_bytes=LIMIT),
        name="fix_late",
    )(slot_grain, value, field, *got_faces, base, out, sums)


def fix_whole(sizes, value, field, got_faces, got_sides, base, out):
    return pl.pallas_call(
        functools.partial(fix_kernel, sizes, "whole"),
        out_shape=[BLOCK, WHOLE],
        in_specs=[VM] * 7 + [HBM],
        out_specs=[VM, HBM],
        scratch_shapes=[EDGE, STORES],
        input_output_aliases={6: 0, 7: 1},
        compiler_params=pltpu.CompilerParams(vmem_limit_bytes=LIMIT),
        name="fix_whole",
    )(value, field, *got_faces, *got_sides, base, out)[1]


def swaps(axis, count, first, second):
    near = [(i, i ^ 1) for i in range(count)]
    far = [(i, ((i + 1) ^ 1) - 1) for i in range(1, count - 1)]
    pairs = far, near
    return lax.ppermute(first, axis, pairs[0]), lax.ppermute(second, axis, pairs[1])


def shards(n_gx, n_gy, cotangent, fields_one, fields_zero, slot_grain):
    sizes = n_gx, n_gy
    cotangent, fields_one, fields_zero = (
        pltpu.with_memory_space_constraint(array, pltpu.HBM)
        for array in (cotangent, fields_one, fields_zero)
    )
    face_a, face_b, side_a, side_b = pack(cotangent)
    first_faces = swaps("gx", n_gx, face_a, face_b)
    got_sides = swaps("gy", n_gy, side_a, side_b)
    out, value, field, base, sums = local_step(cotangent, fields_one)
    base, sums, side_a, side_b = fix_early(sizes, value, field, first_faces, got_sides, base, sums)

    got_sides = swaps("gy", n_gy, side_a, side_b)
    _, costate, _, face_a, face_b, rows = fix_late(
        sizes, slot_grain, value, field, first_faces, base, out, sums
    )
    side_a, side_b, face_a, face_b, corners = corner(
        sizes, first_faces, rows, got_sides, (face_a, face_b)
    )
    got_faces = swaps("gx", n_gx, face_a, face_b)
    got_rows = lax.all_to_all(
        rows.reshape(n_gx, GRAIN_DEV, NZ), "gx", split_axis=0, concat_axis=0, tiled=True
    )
    costate = pltpu.with_memory_space_constraint(costate, pltpu.HBM)
    out, value, field, base = local_step(costate, fields_zero, corners)
    adjoint = fix_whole(sizes, value, field, got_faces, (side_a, side_b), base, out)
    got_rows, adjoint = lax.optimization_barrier((got_rows, adjoint))
    grain_grad = jnp.sum(got_rows.reshape(n_gx, GRAIN_DEV, NZ), axis=0)
    return adjoint, grain_grad


def solution(mesh):
    placed = (
        P(None, "gx", "gy", None),
        P(None, "gx", "gy", None),
        P(None, "gx", "gy", None),
        P("gx", "gy", None),
    )
    return jax.shard_map(
        functools.partial(shards, mesh.shape["gx"], mesh.shape["gy"]),
        mesh=mesh,
        in_specs=placed,
        out_specs=(P(None, "gx", "gy", None), P(("gx", "gy"), None)),
        check_vma=False,
    )
```
